256 devices in a mesh: dp: 4 (over x), ctx: 16 (over z_lo, y), tensor: 4 (over z_hi, core).
Axes of the slice: x: 4, y: 4, z: 8 (z_hi: 2, z_lo: 4; z = z_hi * 4 + z_lo), core: 2. Of those that a mesh axis runs over, the one named last changes fastest.
Arguments:
- queries: bfloat16 [4, 4096, 4, 1024], P('dp', 'ctx', 'tensor'), may hold values from -120 to 120
- keys: bfloat16 [4, 4096, 4, 128], P('dp', 'ctx', 'tensor'), may hold values from -7 to 7
- values: bfloat16 [4, 4096, 4, 128], P('dp', 'ctx', 'tensor'), may hold values from -6 to 6
- student_x: bfloat16 [4, 4096, 4, 1024], P('dp', 'ctx', 'tensor'), may hold values from -12 to 12
- student_bc: bfloat16 [4, 4096, 4, 2, 128], P('dp', 'ctx', 'tensor'), may hold values from -2 to 2
- student_dt: float32 [4, 4096, 4, 16], P('dp', 'ctx', 'tensor'), may hold values from -4 to 4
- a_log: float32 [4, 16], P('tensor'), may hold values from -4 to 2
- dt_bias: float32 [4, 16], P('tensor'), may hold values from -5.5 to -3.5
- skip: float32 [4, 16], P('tensor'), may hold values from 0.5 to 1.5
Outputs:
- grad_x: bfloat16 [4, 4096, 4, 1024], P('dp', 'ctx', 'tensor')
- grad_bc: bfloat16 [4, 4096, 4, 2, 128], P('dp', 'ctx', 'tensor')
- grad_dt: float32 [4, 4096, 4, 16], P('dp', 'ctx', 'tensor')
- grad_heads: float32 [3, 4, 16], P(None, 'tensor')
- loss: float32 [], replicated
The draws below stay inside these ranges and needn't reach their ends.
All inputs are finite; a program needn't handle non-finite values.
Results may differ from the reference program's by a relative error of at most 0.006.
Values may be sent and summed in bfloat16 or wider, within the bound.
A program may use at most 64 MiB of HBM per device.

```python
import jax
import jax.numpy as jnp
from jax import lax

SPAN = 256
HD = 128
GROUP = 8
P_SIZE = 64
N = 128
KV = 4
HG = 16
SEQS = 4
LENGTH = 4096


def teacher_streams(key):
    base = jax.random.fold_in(key, 4099)
    key_query, key_keys = jax.random.split(base, 2)
    key_rows = jnp.clip(jax.random.normal(key_keys, (SEQS, LENGTH, KV, HD), jnp.float32), -6.0, 6.0)
    query_rows = jnp.clip(2.0 * jax.random.normal(key_query, (SEQS, LENGTH, KV, GROUP, HD), jnp.float32), -12.0, 12.0)
    return (query_rows.reshape(SEQS, LENGTH, KV, GROUP * HD), key_rows)


def draw_queries(key, part):
    return teacher_streams(key)[0].astype(jnp.bfloat16)


def draw_keys(key, part):
    return teacher_streams(key)[1].astype(jnp.bfloat16)


def draw_student_x(key, part):
    base = jax.random.fold_in(key, 7717)
    seq_index = jnp.arange(SEQS, dtype=jnp.float32)[:, None]
    place_index = jnp.arange(LENGTH, dtype=jnp.float32)[None, :]
    ramp = (seq_index * LENGTH + place_index) / max(SEQS * LENGTH - 1, 1)
    shape = (SEQS, LENGTH, KV, HG * P_SIZE)
    amplitude = 0.6 * jnp.exp(ramp * jnp.log(3.0))
    noise = jnp.clip(jax.random.normal(base, shape, jnp.float32), -6.0, 6.0)
    return (noise * amplitude[:, :, None, None]).astype(jnp.bfloat16)


def shard_levels(stream_key, extent, shards, low, top_value):
    factor_of, own = 1.0, jax.random.fold_in(stream_key, 6)
    for position, shards_of in shards:
        heights = jnp.exp(jax.random.uniform(jax.random.fold_in(own, position), (shards_of,), jnp.float32, low / len(shards), top_value / len(shards)))
        factor_of = factor_of * jnp.repeat(heights, extent[position] // shards_of).reshape([-1 if axis == position else 1 for axis in range(len(extent))])
    return factor_of


def bell_draw(key, extent, deviation, bound, pieces=(), kind=jnp.bfloat16):
    result = jax.random.normal(key, extent, jnp.float32) * deviation
    if len(pieces) > 0:
        result = shard_levels(key, extent, pieces, -0.22, 0.18) * result
    return jnp.clip(result, min=-bound, max=bound).astype(kind)


def setup_inputs(seed: int = 0) -> dict:
    seeds = jax.random.split(jax.random.key(seed), 10)
    return {
        "queries": draw_queries(jax.random.fold_in(seeds[9], 71), 0),
        "keys": draw_keys(jax.random.fold_in(seeds[9], 71), 0),
        "values": bell_draw(seeds[2], (SEQS, LENGTH, KV, HD), 1.0, 6.0, ((0, 4), (1, 16), (2, 4))),
        "student_x": draw_student_x(jax.random.fold_in(seeds[9], 71), 0),
        "student_bc": bell_draw(seeds[4], (SEQS, LENGTH, KV, 2, N), 0.3, 2.0, ((0, 4), (1, 16), (2, 4))),
        "student_dt": bell_draw(seeds[5], (SEQS, LENGTH, KV, HG), 1.0, 4.0, ((0, 4), (1, 16), (2, 4)), jnp.float32),
        "a_log": jnp.clip(-4.0 + 6.0 * jax.random.uniform(seeds[6], (KV, HG), jnp.float32) ** shard_levels(seeds[6], (KV, HG), ((0, 4),), -0.2, 0.2), -4.0, 2.0),
        "dt_bias": jnp.clip(-5.5 + 2.0 * jax.random.uniform(seeds[7], (KV, HG), jnp.float32) ** shard_levels(seeds[7], (KV, HG), ((0, 4),), -0.2, 0.2), -5.5, -3.5),
        "skip": jnp.clip(0.5 + 1.0 * jax.random.uniform(seeds[8], (KV, HG), jnp.float32) ** shard_levels(seeds[8], (KV, HG), ((0, 4),), -0.2, 0.2), 0.5, 1.5),
    }


HIGH = lax.Precision.HIGHEST
EPSILON = 1e-06

def teacher_sequence(queries, keys, values):
    length = queries.shape[0]
    block_rows = min(512, length)
    block_count = length // block_rows

    def per_group(items):
        query_group, key_group, value_group = items
        query_blocks = query_group.reshape(block_count, block_rows, GROUP, HD).astype(jnp.float32)
        key_values = key_group.astype(jnp.float32)
        value_rows = value_group.astype(jnp.float32)
        block_starts = jnp.arange(block_count, dtype=jnp.int32) * block_rows

        def per_block(pair):
            query_block, block_start = pair
            scores = jnp.einsum('qgd,kd->gqk', query_block, key_values) * HD ** (-0.5)
            query_places = block_start + jnp.arange(block_rows, dtype=jnp.int32)
            allowed = (jnp.arange(length, dtype=jnp.int32)[None, :] <= query_places[:, None])[None]
            scores = jnp.where(allowed, scores, -jnp.inf)
            largest = lax.optimization_barrier(jnp.max(scores, axis=-1, keepdims=True))
            weights = jnp.exp(scores - largest)
            totals = lax.optimization_barrier(jnp.sum(weights, axis=-1))
            rounded = lax.optimization_barrier(weights.astype(jnp.bfloat16)).astype(jnp.float32)
            mixed = jnp.einsum('gqk,kd->qgd', rounded, value_rows)
            return (mixed / totals.T[:, :, None]).astype(jnp.bfloat16)
        outcome = lax.map(per_block, (query_blocks, block_starts))
        return outcome.reshape(length, GROUP * HD)
    grouped = lax.map(per_group, (jnp.transpose(queries, (1, 0, 2)), jnp.transpose(keys, (1, 0, 2)), jnp.transpose(values, (1, 0, 2))))
    return jnp.transpose(grouped, (1, 0, 2))

def teacher_item(items):
    return teacher_sequence(items[0], items[1], items[2])

def student_sequence(inputs, pairs, raw_rate, log_rate, bias_rate, skip_rate):
    length = inputs.shape[0]
    block_count = length // SPAN
    heads = inputs.reshape(block_count, SPAN, KV, HG, P_SIZE)
    b_rows = pairs[:, :, 0].reshape(block_count, SPAN, KV, N)
    c_rows = pairs[:, :, 1].reshape(block_count, SPAN, KV, N)
    step_size = jax.nn.softplus(raw_rate + bias_rate).reshape(block_count, SPAN, KV, HG)
    decay_step = -step_size * jnp.exp(log_rate)
    lower = jnp.arange(SPAN)[:, None] >= jnp.arange(SPAN)[None, :]
    masked = lower[:, :, None, None]

    def advance(carried, items):
        span_in, b_span, c_span, size_span, decay_span = items
        cumulative = jnp.cumsum(decay_span, axis=0)
        spread = cumulative[:, None] - cumulative[None, :]
        decays = jnp.where(masked, jnp.exp(jnp.where(masked, spread, 0.0)), 0.0)
        intersection = jnp.einsum('tgn,sgn->tsg', c_span, b_span, precision=HIGH)
        mixing = decays * size_span[None] * intersection[..., None]
        intra = jnp.einsum('tsgh,sghp->tghp', mixing, span_in, precision=HIGH)
        inter = jnp.exp(cumulative)[..., None] * jnp.einsum('ghpn,tgn->tghp', carried, c_span, precision=HIGH)
        output = intra + inter + skip_rate[..., None] * span_in
        tail = jnp.exp(cumulative[-1][None] - cumulative)
        updated = jnp.exp(cumulative[-1])[..., None, None] * carried + jnp.einsum('sgh,sghp,sgn->ghpn', tail * size_span, span_in, b_span, precision=HIGH)
        return (updated, output)
    initial = jnp.zeros((KV, HG, P_SIZE, N), jnp.float32)
    final_state, outputs = lax.scan(jax.checkpoint(advance), initial, (heads, b_rows, c_rows, step_size, decay_step))
    return outputs.reshape(length, KV, HG * P_SIZE)

def reference(queries, keys, values, student_x, student_bc, student_dt, a_log, dt_bias, skip):
    targets = lax.map(teacher_item, (queries, keys, values))
    target_values = targets.astype(jnp.float32)
    entries = target_values.size
    mean_square = jnp.sum(target_values * target_values) / entries + EPSILON

    def alignment(inputs, pairs, raw_rate, log_rate, bias_rate, skip_rate):

        def per_sequence(items):
            seq_inputs, seq_pairs, seq_raw, seq_target = items
            output = student_sequence(seq_inputs, seq_pairs, seq_raw, log_rate, bias_rate, skip_rate)
            residual = output - seq_target
            return jnp.sum(residual * residual)
        return jnp.sum(lax.map(per_sequence, (inputs, pairs, raw_rate, target_values))) / mean_square
    value, pullback = jax.vjp(alignment, student_x.astype(jnp.float32), student_bc.astype(jnp.float32), student_dt, a_log, dt_bias, skip)
    grads = pullback(jnp.ones((), jnp.float32))
    grad_heads = jnp.stack([grads[3], grads[4], grads[5]])
    return (grads[0].astype(jnp.bfloat16), grads[1].astype(jnp.bfloat16), grads[2], grad_heads, value / entries)
```

```python
import jax
import jax.numpy as jnp
from jax import lax
from jax.experimental import pallas as pl
from jax.experimental.pallas import tpu as pltpu
from jax.sharding import PartitionSpec as P

T = 256
HD = 128
GROUP = 8
N = 128
HG = 16
CH = 1024
QW = 256
ROW = 4
F32 = jnp.float32
BF16 = jnp.bfloat16
NEGATIVE = -1e30
EPSILON = 1e-06
EXP_SCALE = 1.4426950408889634 * HD**-0.5
MESH = pl.DeviceIdType.MESH


def nn(a, b):
    return lax.dot_general(a, b, (((1,), (0,)), ((), ())), preferred_element_type=F32)


def nt(a, b):
    return lax.dot_general(a, b, (((1,), (1,)), ((), ())), preferred_element_type=F32)


def tn(a, b):
    return lax.dot_general(a, b, (((0,), (0,)), ((), ())), preferred_element_type=F32)


def pieces(a, count):
    out = []
    for _ in range(count - 1):
        top = a.astype(BF16)
        out.append(top)
        a = a - top.astype(F32)
    out.append(a.astype(BF16))
    return out


def summed(form, values, marks, count=3, left=True):
    total = None
    for part in pieces(values, count):
        term = form(part, marks) if left else form(marks, part)
        total = term if total is None else total + term
    return total


def iota(shape, dim):
    return lax.broadcasted_iota(jnp.int32, shape, dim)


def marks(shape, test):
    return jnp.where(test(iota(shape, 0), iota(shape, 1)), 1.0, 0.0).astype(BF16)


def column(ref):
    wide = jnp.broadcast_to(ref[...], (HG, HG))
    same = iota((HG, HG), 0) == iota((HG, HG), 1)
    return jnp.sum(jnp.where(same, wide, 0.0), axis=1, keepdims=True)


def kernel(
    entries, dp_size, tensor_size,
    q, k, v, x, bc, dt, alog, dtb, skp,
    gx, gbc, gdt, ghd, gls,
    kbuf, vbuf, m_ref, acc, timed, mixt, cumb, stepb, cumt, stept, wmat, wtmat,
    intra, inter, upb, ups, ts_full, ecum_full, xs, eu, t1,
    tot, tq,
    ysend, yrecv, zsend, zrecv, bsend, brecv,
    ysend2, yrecv2, zsend2, zrecv2, bsend2, brecv2,
    sy, sz, sd, st, hy, hz, hd,
    own_sem, kv_recv, kvz_send, kvy_send,
    tot_send, tot_recv, scan_send, scan_recv, red_send, red_recv,
):
    c = lax.axis_index("ctx")
    d = lax.axis_index("dp")
    tt = lax.axis_index("tensor")
    z = c // ROW
    y = c % ROW

    def at_y(step):
        return {"ctx": z * ROW + (y + step) % ROW}

    def at_z(step):
        return {"ctx": ((z + step) % ROW) * ROW + y}

    def at_d(step):
        return {"dp": (d + step) % dp_size}

    def at_t(step):
        return {"tensor": (tt + step) % tensor_size}

    peers = [at_y(s) for s in range(1, ROW)] + [at_z(s) for s in range(1, ROW)]
    peers += [at_d(s) for s in range(1, dp_size)] + [at_t(s) for s in range(1, tensor_size)]

    zrecv[...] = jnp.zeros_like(zrecv)
    zrecv2[...] = jnp.zeros_like(zrecv2)

    barrier = pltpu.get_barrier_semaphore()
    for peer in peers:
        pl.semaphore_signal(barrier, inc=1, device_id=peer, device_id_type=MESH)

    def rows(slot):
        return pl.ds(pl.multiple_of(slot * T, T), T)

    own_k = pltpu.make_async_copy(k, kbuf.at[rows(c)], own_sem.at[0])
    own_v = pltpu.make_async_copy(v, vbuf.at[rows(c)], own_sem.at[1])
    own_k.start()
    own_v.start()
    pl.semaphore_wait(barrier, len(peers))

    def remote(src, dst, send, recv, peer):
        return pltpu.make_async_remote_copy(
            src_ref=src, dst_ref=dst, send_sem=send, recv_sem=recv,
            device_id=peer, device_id_type=MESH,
        )

    bufs = (kbuf, vbuf)

    def kv_z(step, which):
        return remote(
            (k, v)[which], bufs[which].at[rows(c)], kvz_send.at[step - 1, which],
            kv_recv.at[which, c], at_z(step),
        )

    def kv_y(back, lane, which, slot, step):
        return remote(
            bufs[which].at[rows(slot)], bufs[which].at[rows(slot)], kvy_send.at[back, lane],
            kv_recv.at[which, slot], at_y(step),
        )

    def kv_wait(which, slot):
        remote(
            bufs[which].at[rows(slot)], bufs[which].at[rows(slot)], own_sem.at[which],
            kv_recv.at[which, slot], at_y(1),
        ).wait_recv()

    def y_sends(back):
        slot = (z - back) * ROW + y
        return [
            kv_y(back, 0, 0, slot, 1), kv_y(back, 1, 1, slot, 3),
            kv_y(back, 2, 1, slot, 1), kv_y(back, 3, 0, slot, 3),
        ]

    def slot_of(back, step):
        return (z - back) * ROW + (y + step) % ROW

    def forwards(back):
        return [kv_y(back, 4, 0, slot_of(back, 3), 1), kv_y(back, 5, 1, slot_of(back, 1), 3)]

    for step in (3, 2, 1):

        @pl.when(z + step < ROW)
        def _():
            for which in range(2):
                kv_z(step, which).start()

    own_k.wait()
    own_v.wait()
    for copy in y_sends(0):
        copy.start()

    def pass_down(back):
        for which in range(2):
            kv_wait(which, slot_of(back, 0))
        for copy in y_sends(back):
            copy.start()

    def pass_on(back):
        kv_wait(0, slot_of(back, 3))
        kv_wait(1, slot_of(back, 1))
        for copy in forwards(back):
            copy.start()

    def settle(back):
        kv_wait(1, slot_of(back, 3))
        kv_wait(0, slot_of(back, 1))
        for which in range(2):
            kv_wait(which, slot_of(back, 2))

    bias = column(dtb)
    rate = jnp.exp(column(alog))
    shifted = dt[...] + bias
    step_size = jnp.maximum(shifted, 0.0) + jnp.log1p(jnp.exp(-jnp.abs(shifted)))
    decay = -step_size * rate
    upto = marks((T, T), lambda s, t: s <= t)
    same = marks((T, T), lambda s, t: s == t)
    cum_t = summed(nn, decay, upto)
    cum_c = summed(nt, cum_t, same, left=False)
    total = cum_t[:, T - 1 : T]
    cumt[...] = cum_t
    stept[...] = step_size
    spread = marks((HG, CH), lambda h, j: (j >> 6) == h)
    tail_step = jnp.exp(total - cum_t) * step_size
    ts_full[...] = summed(tn, tail_step, spread, 2)
    xs[...] = (ts_full[...] * x[...].astype(F32)).astype(BF16)
    pick_b = marks((T, 2 * T), lambda t, r: r == 2 * t)
    pick_c = marks((T, 2 * T), lambda t, r: r == 2 * t + 1)
    b_f = nn(pick_b, bc[...])
    c_f = nn(pick_c, bc[...])
    b_rows = b_f.astype(BF16)
    c_rows = c_f.astype(BF16)
    b_cols = b_f.T.astype(BF16)
    c_cols = c_f.T.astype(BF16)

    tot[pl.ds(c, 1)] = jnp.broadcast_to(
        jnp.concatenate([cum_c[T - 1 : T, :], jnp.zeros((1, 128 - HG), F32)], axis=1)[None],
        (1, 8, 128),
    )
    for part in range(4):
        ysend[part] = nn(b_cols, xs[:, part * QW : (part + 1) * QW]).astype(BF16)

    def tot_y(step):
        return remote(
            tot.at[pl.ds(c, 1)], tot.at[pl.ds(c, 1)], tot_send.at[0, step - 1],
            tot_recv.at[0, y], at_y(step),
        )

    def tot_y_wait(step):
        other = (y + step) % ROW
        remote(
            tot.at[pl.ds(c, 1)], tot.at[pl.ds(z * ROW + other, 1)], tot_send.at[0, step - 1],
            tot_recv.at[0, other], at_y(step),
        ).wait_recv()

    def tot_z(step):
        return remote(
            tot.at[pl.ds(z * ROW, ROW)], tot.at[pl.ds(z * ROW, ROW)], tot_send.at[1, step - 1],
            tot_recv.at[1, z], at_z(step),
        )

    def tot_z_wait(step):
        other = (z + step) % ROW
        remote(
            tot.at[pl.ds(z * ROW, ROW)], tot.at[pl.ds(other * ROW, ROW)], tot_send.at[1, step - 1],
            tot_recv.at[1, other], at_z(step),
        ).wait_recv()

    def trade(phase, src, dst, step):
        to = (y + step) % ROW
        return remote(
            src.at[to], dst.at[y], scan_send.at[phase, step - 1], scan_recv.at[phase, y], at_y(step)
        )

    def trade_wait(phase, src, dst, step):
        other = (y + step) % ROW
        remote(
            src.at[other], dst.at[other], scan_send.at[phase, step - 1],
            scan_recv.at[phase, other], at_y(step),
        ).wait_recv()

    def climb(phase, src, dst, step):
        return remote(src, dst.at[z], scan_send.at[phase, step - 1], scan_recv.at[phase, z], at_z(step))

    def climb_wait(phase, src, dst, step):
        other = (z + step) % ROW
        remote(
            src, dst.at[other], scan_send.at[phase, step - 1], scan_recv.at[phase, other], at_z(step)
        ).wait_recv()

    for step in range(1, ROW):
        tot_y(step).start()
    for step in range(1, ROW):
        trade(0, ysend, yrecv, step).start()
    yrecv[pl.ds(y, 1)] = ysend[pl.ds(y, 1)]

    wmat[...] = nt(c_rows, b_rows)
    wtmat[...] = nt(b_rows, c_rows)
    wide = marks((HG, HG * 128), lambda h, j: (j >> 7) == h)
    cumb[...] = summed(tn, cum_t, wide)
    stepb[...] = summed(tn, step_size, wide)
    ecum_full[...] = summed(tn, jnp.exp(cum_t), spread, 2)

    for step in range(1, ROW):
        tot_y_wait(step)
    for step in range(1, ROW):
        tot_z(step).start()

    low_half = iota((T, 128), 1) < 64
    zero_pair = jnp.zeros((T, 128), BF16)

    def halves(pair):
        return jnp.where(low_half, pair, zero_pair), jnp.where(low_half, zero_pair, pair)

    def lanes(index, width):
        return pl.ds(pl.multiple_of(index * width, width), width)

    def mix_pair(pair, carry):
        lower = iota((T, T), 0) >= iota((T, T), 1)
        upper = iota((T, T), 0) <= iota((T, T), 1)
        parts = halves(x[:, lanes(pair, 128)])
        result = jnp.zeros((T, 128), F32)
        for i in range(2):
            h = 2 * pair + i
            at_t = cumb[:, lanes(h, 128)]
            at_t = jnp.concatenate([at_t, at_t], axis=1)
            size_c = stepb[:, lanes(h, 128)]
            size_c = jnp.concatenate([size_c, size_c], axis=1)
            at_s = cumt[pl.ds(h, 1), :]
            size_r = stept[pl.ds(h, 1), :]
            held = jnp.exp(jnp.where(lower, at_t - at_s, NEGATIVE)) * size_r
            timed[h] = held
            mixed = (held * wmat[...]).astype(BF16)
            result = result + nn(mixed, parts[i])
            turned = jnp.exp(jnp.where(upper, at_s - at_t, NEGATIVE)) * size_c
            mixt[h] = (turned * wtmat[...]).astype(BF16)
        intra[:, lanes(pair, 128)] = result
        return carry

    @pl.when(z >= 1)
    def _():
        pass_down(1)

    lax.fori_loop(0, GROUP, mix_pair, 0)
    pass_on(0)

    tot_all_ready = [tot_z_wait(step) for step in range(1, ROW)]
    del tot_all_ready
    totals = jnp.sum(jnp.where(iota((16, 8, 128), 1) == 0, tot[...], 0.0), axis=1)
    mine = marks((128, QW), lambda h, j: h == y * 4 + (j >> 6))
    tq[...] = summed(nn, totals, mine)

    def total_of(zz, kk):
        return tq[pl.ds(zz * ROW + kk, 1), :]

    def row_total(zz):
        return total_of(zz, 0) + total_of(zz, 1) + total_of(zz, 2) + total_of(zz, 3)

    def scan_row(phase, src, got, up, order):
        for step in range(1, ROW):
            trade_wait(phase, src, got, step)
        run = jnp.zeros((N, QW), F32)
        before = {}
        for kk in order:
            before[kk] = run
            run = jnp.exp(total_of(z, kk)) * run + got[kk].astype(F32)
        up[...] = run.astype(BF16)
        return before

    def scan_back(phase, got, back, final, before, order, rows_in, arrived):
        held = jnp.zeros((N, QW), F32)
        for zz in rows_in:
            held = jnp.where(
                arrived(zz), jnp.exp(row_total(zz)) * held + got[zz].astype(F32), held
            )
        passed = jnp.zeros((1, QW), F32)
        for kk in order:
            back[kk] = (jnp.exp(passed) * held + before[kk]).astype(BF16)
            passed = passed + total_of(z, kk)
        for step in range(1, ROW):
            trade(phase, back, final, step).start()
        final[pl.ds(y, 1)] = back[pl.ds(y, 1)]

    ahead = (0, 1, 2, 3)
    behind = (3, 2, 1, 0)
    before = scan_row(0, ysend, yrecv, zsend, ahead)
    for step in range(1, ROW):

        @pl.when(z + step < ROW)
        def _():
            climb(1, zsend, zrecv, step).start()

    ones = jnp.ones((ROW * T, HD), BF16)

    def attend(back, first):
        base = pl.multiple_of((z - back) * (ROW * T), ROW * T)

        def one(g, carry):
            keys = kbuf[pl.ds(base, ROW * T), :]
            both = jnp.concatenate([vbuf[pl.ds(base, ROW * T), :], ones], axis=1)
            scores = nt(q[:, lanes(g, HD)], keys)
            if first:
                seen = iota((T, ROW * T), 1) <= iota((T, ROW * T), 0) + y * T
                scores = jnp.where(seen, scores, NEGATIVE)
            top = jnp.max(scores, axis=1, keepdims=True)
            if first:
                new = jnp.broadcast_to(top, (T, HD))
            else:
                old = m_ref[g]
                new = jnp.maximum(old, top)
            weights = jnp.exp2((scores - jnp.concatenate([new] * 8, axis=1)) * EXP_SCALE)
            part = nn(weights.astype(BF16), both)
            if first:
                acc[g] = part
            else:
                scale = jnp.exp2((old - new) * EXP_SCALE)
                acc[g] = acc[g] * jnp.concatenate([scale, scale], axis=1) + part
            m_ref[g] = new
            return carry

        lax.fori_loop(0, GROUP, one, 0)

    @pl.when(z >= 2)
    def _():
        pass_down(2)

    settle(0)
    attend(0, True)

    @pl.when(z >= 1)
    def _():
        pass_on(1)

    for step in range(1, ROW):

        @pl.when(z >= step)
        def _():
            climb_wait(1, zsend, zrecv, ROW - step)

    scan_back(2, zrecv, bsend, brecv, before, ahead, (0, 1, 2), lambda zz: zz < z)

    @pl.when(z >= 3)
    def _():
        pass_down(3)

    @pl.when(z >= 1)
    def _():
        settle(1)
        attend(1, False)

    @pl.when(z >= 2)
    def _():
        pass_on(2)

    @pl.when(z >= 3)
    def _():
        pass_on(3)

    for step in range(1, ROW):
        trade_wait(2, bsend, brecv, step)
    for part in range(4):
        cut = slice(part * QW, (part + 1) * QW)
        inter[:, cut] = ecum_full[:, cut] * nn(c_rows, brecv[part])

    for back in (2, 3):

        @pl.when(z >= back)
        def _():
            settle(back)
            attend(back, False)

    skip_row = summed(nn, jnp.broadcast_to(skp[...], (8, HG)), spread)[0:1, :]

    def fold(a):
        a = a.reshape(T // 8, 8, a.shape[1])
        a = jnp.sum(a, axis=0)
        out = a[:, 0:128]
        for j in range(1, a.shape[1] // 128):
            out = out + a[:, j * 128 : (j + 1) * 128]
        return out

    power = jnp.zeros((8, 128), F32)
    error = jnp.zeros((8, 128), F32)
    for g in range(GROUP):
        cut = slice(g * 128, (g + 1) * 128)
        both = acc[g]
        goal = (both[:, :HD] / both[:, HD:]).astype(BF16).astype(F32)
        made = intra[:, cut] + inter[:, cut] + skip_row[:, cut] * x[:, cut].astype(F32)
        resid = made - goal
        power = power + fold(goal * goal)
        error = error + fold(resid * resid)
        up = 2.0 * resid
        ups[:, cut] = up
        upb[:, cut] = up.astype(BF16)
        eu[:, cut] = (ecum_full[:, cut] * up).astype(BF16)
    for part in range(4):
        ysend2[part] = nn(c_cols, eu[:, part * QW : (part + 1) * QW]).astype(BF16)
    for step in range(1, ROW):
        trade(3, ysend2, yrecv2, step).start()
    yrecv2[pl.ds(y, 1)] = ysend2[pl.ds(y, 1)]

    def spread_out(buf, place, stage, at, size):
        out = []
        for step in range(1, size):
            out.append(
                remote(
                    buf.at[pl.ds(place, 1)], buf.at[pl.ds(place, 1)], red_send.at[stage, step - 1],
                    red_recv.at[stage, place], at(step),
                )
            )
        return out

    def collect(buf, place, stage, at, size):
        for step in range(1, size):
            other = (place + step) % size
            remote(
                buf.at[pl.ds(place, 1)], buf.at[pl.ds(other, 1)], red_send.at[stage, step - 1],
                red_recv.at[stage, other], at(step),
            ).wait_recv()
        total = buf[0]
        for j in range(1, size):
            total = total + buf[j]
        return total

    def launch(value, buf, place, stage, at, size):
        buf[pl.ds(place, 1)] = value[None]
        for copy in spread_out(buf, place, stage, at, size):
            copy.start()

    launch(jnp.concatenate([power, error], axis=0), sy, y, 0, at_y, ROW)

    before2 = scan_row(3, ysend2, yrecv2, zsend2, behind)
    for step in range(1, ROW):

        @pl.when(z >= step)
        def _():
            climb(4, zsend2, zrecv2, ROW - step).start()

    launch(collect(sy, y, 0, at_y, ROW), sz, z, 1, at_z, ROW)

    def pair_products(pair, running):
        ups_pair = halves(upb[:, lanes(pair, 128)])
        x_pair = x[:, lanes(pair, 128)]
        through = jnp.zeros((T, 128), F32)
        for i in range(2):
            h = 2 * pair + i
            running = running + timed[h] * nt(ups_pair[i], x_pair)
            through = through + nn(mixt[h], ups_pair[i])
        t1[:, lanes(pair, 128)] = through
        return running

    paired = lax.fori_loop(0, GROUP // 2, pair_products, jnp.zeros((T, T), F32))
    launch(collect(sz, z, 1, at_z, ROW), sd, d, 2, at_d, dp_size)
    for step in range(1, ROW):

        @pl.when(z + step < ROW)
        def _():
            climb_wait(4, zsend2, zrecv2, step)

    scan_back(5, zrecv2, bsend2, brecv2, before2, behind, (3, 2, 1), lambda zz: zz > z)
    paired = lax.fori_loop(GROUP // 2, GROUP, pair_products, paired)
    launch(collect(sd, d, 2, at_d, dp_size), st, tt, 3, at_t, tensor_size)

    paired_rows = paired.astype(BF16)
    paired_cols = paired.T.astype(BF16)
    grad_b = nn(paired_cols, c_rows)
    grad_c = nn(paired_rows, b_rows)
    for part in range(4):
        grad_c = grad_c + nt(eu[:, part * QW : (part + 1) * QW], brecv[part])

    def by_head(a):
        return summed(nt, a, spread, 2, left=False)

    xf = x[...].astype(F32)
    gained = by_head(upb[...].astype(F32) * intra[...] - xf * t1[...]) + by_head(
        ups[...] * inter[...]
    )
    from_mix = by_head(xf * t1[...])
    skip_term = jnp.sum(by_head(ups[...] * xf), axis=1, keepdims=True)
    since = marks((T, T), lambda s, t: s >= t)
    until = marks((T, T), lambda s, t: s < t)
    gained_after = summed(nn, gained, since)
    gate = 1.0 / (1.0 + jnp.exp(-shifted))

    both_sums = collect(st, tt, 3, at_t, tensor_size)
    power_all = jnp.sum(both_sums[0:8, :], keepdims=True)
    error_all = jnp.sum(both_sums[8:16, :], keepdims=True)
    mean_square = power_all / entries + EPSILON
    factor = 1.0 / mean_square
    gls[...] = jnp.broadcast_to(error_all / mean_square / entries, (8, 128))

    for step in range(1, ROW):
        trade_wait(5, bsend2, brecv2, step)
    overlap = []
    for part in range(4):
        cut = slice(part * QW, (part + 1) * QW)
        later = brecv2[part]
        inter[:, cut] = ts_full[:, cut] * nn(b_rows, later)
        prod = later.astype(F32) * brecv[part].astype(F32)
        overlap.append(jnp.sum(prod.reshape(N // 8, 8, QW), axis=0))
    from_later = by_head(xf * inter[...])
    meet = jnp.sum(by_head(jnp.concatenate(overlap, axis=1)), axis=1, keepdims=True)
    decay_grad = gained_after + summed(nn, from_later, until) + jnp.exp(total) * meet
    direct = (from_mix + from_later) / step_size
    shift_grad = (direct - decay_grad * rate) * gate
    decay_term = jnp.sum(decay_grad * decay, axis=1, keepdims=True)
    shift_term = jnp.sum(shift_grad, axis=1, keepdims=True)
    lane = iota((HG, 128), 1)
    heads = jnp.where(lane == 0, decay_term, jnp.where(lane == 1, shift_term, skip_term))
    launch(heads, hy, y, 4, at_y, ROW)
    gdt[...] = shift_grad * factor
    for part in range(4):
        grad_b = grad_b + nt(xs[:, part * QW : (part + 1) * QW], brecv2[part])
    launch(collect(hy, y, 4, at_y, ROW), hz, z, 5, at_z, ROW)
    put_b = marks((2 * T, T), lambda r, t: r == 2 * t)
    put_c = marks((2 * T, T), lambda r, t: r == 2 * t + 1)
    gbc[...] = (
        nn(put_b, (grad_b * factor).astype(BF16)) + nn(put_c, (grad_c * factor).astype(BF16))
    ).astype(BF16)
    launch(collect(hz, z, 5, at_z, ROW), hd, d, 6, at_d, dp_size)
    gx[...] = ((skip_row * ups[...] + t1[...] + inter[...]) * factor).astype(BF16)
    ghd[...] = collect(hd, d, 6, at_d, dp_size) * factor

    for step in range(1, ROW):

        @pl.when(z + step < ROW)
        def _():
            for which in range(2):
                kv_z(step, which).wait_send()
            climb(1, zsend, zrecv, step).wait_send()

        @pl.when(z >= step)
        def _():
            climb(4, zsend2, zrecv2, ROW - step).wait_send()

        tot_y(step).wait_send()
        tot_z(step).wait_send()
        trade(0, ysend, yrecv, step).wait_send()
        trade(2, bsend, brecv, step).wait_send()
        trade(3, ysend2, yrecv2, step).wait_send()
        trade(5, bsend2, brecv2, step).wait_send()
    for back in range(ROW):

        @pl.when(z >= back)
        def _():
            for copy in y_sends(back) + forwards(back):
                copy.wait_send()

    for buf, place, stage, at, size in (
        (sy, y, 0, at_y, ROW), (sz, z, 1, at_z, ROW), (sd, d, 2, at_d, dp_size),
        (st, tt, 3, at_t, tensor_size), (hy, y, 4, at_y, ROW), (hz, z, 5, at_z, ROW),
        (hd, d, 6, at_d, dp_size),
    ):
        for copy in spread_out(buf, place, stage, at, size):
            copy.wait_send()


def solution(mesh):
    dp_size, tensor_size = mesh.shape["dp"], mesh.shape["tensor"]
    entries = float(dp_size * mesh.shape["ctx"] * tensor_size * T * CH)

    def vm(shape, kind):
        return pltpu.VMEM(shape, kind)

    chunk4 = (ROW, N, QW)
    scratch = [
        vm((16 * T, HD), BF16), vm((16 * T, HD), BF16),
        vm((GROUP, T, HD), F32), vm((GROUP, T, 2 * HD), F32),
        vm((HG, T, T), F32), vm((HG, T, T), BF16),
        vm((T, HG * 128), F32), vm((T, HG * 128), F32),
        vm((HG, T), F32), vm((HG, T), F32), vm((T, T), F32), vm((T, T), F32),
        vm((T, CH), F32), vm((T, CH), F32), vm((T, CH), BF16), vm((T, CH), F32),
        vm((T, CH), F32), vm((T, CH), F32), vm((T, CH), BF16), vm((T, CH), BF16),
        vm((T, CH), F32),
        vm((16, 8, 128), F32), vm((16, QW), F32),
    ]
    for _ in range(2):
        scratch += [
            vm(chunk4, BF16), vm(chunk4, BF16), vm((N, QW), BF16), vm(chunk4, BF16),
            vm(chunk4, BF16), vm(chunk4, BF16),
        ]
    scratch += [
        vm((ROW, 16, 128), F32), vm((ROW, 16, 128), F32), vm((dp_size, 16, 128), F32),
        vm((tensor_size, 16, 128), F32), vm((ROW, 16, 128), F32), vm((ROW, 16, 128), F32),
        vm((dp_size, 16, 128), F32),
    ]
    sem = pltpu.SemaphoreType.DMA
    scratch += [
        sem((2,)), sem((2, 16)), sem((3, 2)), sem((4, 6)),
        sem((2, 3)), sem((2, 4)), sem((6, 3)), sem((6, 4)), sem((7, 3)), sem((7, 4)),
    ]

    def body(queries, keys, values, student_x, student_bc, student_dt, a_log, dt_bias, skip):
        whole = pl.BlockSpec(memory_space=pltpu.VMEM)

        def run(*refs):
            kernel(entries, dp_size, tensor_size, *refs)

        gx, gbc, gdt, ghd, gls = pl.pallas_call(
            run,
            out_shape=(
                jax.ShapeDtypeStruct((T, CH), BF16),
                jax.ShapeDtypeStruct((2 * T, N), BF16),
                jax.ShapeDtypeStruct((HG, T), F32),
                jax.ShapeDtypeStruct((HG, 128), F32),
                jax.ShapeDtypeStruct((8, 128), F32),
            ),
            in_specs=[whole] * 9,
            out_specs=(whole,) * 5,
            scratch_shapes=scratch,
            compiler_params=pltpu.CompilerParams(
                collective_id=0, has_side_effects=True, vmem_limit_bytes=60 * 1024 * 1024
            ),
            name="align",
        )(
            queries.reshape(T, CH), keys.reshape(T, HD), values.reshape(T, HD),
            student_x.reshape(T, CH), student_bc.reshape(2 * T, N),
            student_dt.reshape(T, HG).T, a_log, dt_bias, skip,
        )
        return (
            gx.reshape(1, T, 1, CH),
            gbc.reshape(1, T, 1, 2, N),
            gdt.T.reshape(1, T, 1, HG),
            ghd[:, :3].T.reshape(3, 1, HG),
            gls[0, 0],
        )

    return jax.shard_map(
        body,
        mesh=mesh,
        in_specs=(
            P("dp", "ctx", "tensor", None),
            P("dp", "ctx", "tensor", None),
            P("dp", "ctx", "tensor", None),
            P("dp", "ctx", "tensor", None),
            P("dp", "ctx", "tensor", None, None),
            P("dp", "ctx", "tensor", None),
            P("tensor", None),
            P("tensor", None),
            P("tensor", None),
        ),
        out_specs=(
            P("dp", "ctx", "tensor", None),
            P("dp", "ctx", "tensor", None, None),
            P("dp", "ctx", "tensor", None),
            P(None, "tensor", None),
            P(),
        ),
        check_vma=False,
    )
```

```python
import jax
import jax.numpy as jnp
from jax import lax
from jax.experimental import pallas as pl
from jax.experimental.pallas import tpu as pltpu
from jax.sharding import PartitionSpec as P

T = 256
HD = 128
GROUP = 8
N = 128
HG = 16
CH = 1024
QW = 256
ROW = 4
F32 = jnp.float32
BF16 = jnp.bfloat16
NEGATIVE = -1e30
EPSILON = 1e-06
EXP_SCALE = 1.4426950408889634 * HD**-0.5
MESH = pl.DeviceIdType.MESH


def nn(a, b):
    return lax.dot_general(a, b, (((1,), (0,)), ((), ())), preferred_element_type=F32)


def nt(a, b):
    return lax.dot_general(a, b, (((1,), (1,)), ((), ())), preferred_element_type=F32)


def tn(a, b):
    return lax.dot_general(a, b, (((0,), (0,)), ((), ())), preferred_element_type=F32)


def pieces(a, count):
    out = []
    for _ in range(count - 1):
        top = a.astype(BF16)
        out.append(top)
        a = a - top.astype(F32)
    out.append(a.astype(BF16))
    return out


def summed(form, values, marks, count=3, left=True):
    total = None
    for part in pieces(values, count):
        term = form(part, marks) if left else form(marks, part)
        total = term if total is None else total + term
    return total


def iota(shape, dim):
    return lax.broadcasted_iota(jnp.int32, shape, dim)


def marks(shape, test):
    return jnp.where(test(iota(shape, 0), iota(shape, 1)), 1.0, 0.0).astype(BF16)


def column(ref):
    wide = jnp.broadcast_to(ref[...], (HG, HG))
    same = iota((HG, HG), 0) == iota((HG, HG), 1)
    return jnp.sum(jnp.where(same, wide, 0.0), axis=1, keepdims=True)


def kernel(
    entries, dp_size, tensor_size,
    q_in, k, v, x_in, bc_in, dt_in, alog, dtb, skp,
    gx, gbc, gdt, ghd, gls,
    q, x, bc, dt, kbuf, vbuf, m_ref, acc, timed, mixt, cumb, stepb, cumt, stept, wmat, wtmat,
    intra, inter, upb, ups, ts_full, ecum_full, xs, eu, t1,
    tot, tq, before,
    ysend, yrecv, zsend, zrecv, bsend, brecv,
    ysend2, yrecv2, zsend2, zrecv2, bsend2, brecv2,
    sy, sz, sd, st, hy, hz, hd,
    own_sem, kv_recv, kvz_send, kvy_send,
    tot_send, tot_recv, scan_send, scan_recv, red_send, red_recv,
):
    c = lax.axis_index("ctx")
    d = lax.axis_index("dp")
    tt = lax.axis_index("tensor")
    z = c // ROW
    y = c % ROW

    def at_y(step):
        return {"ctx": z * ROW + (y + step) % ROW}

    def at_z(step):
        return {"ctx": ((z + step) % ROW) * ROW + y}

    def at_d(step):
        return {"dp": (d + step) % dp_size}

    def at_t(step):
        return {"tensor": (tt + step) % tensor_size}

    peers = [at_y(s) for s in range(1, ROW)] + [at_z(s) for s in range(1, ROW)]
    peers += [at_d(s) for s in range(1, dp_size)] + [at_t(s) for s in range(1, tensor_size)]

    zrecv[...] = jnp.zeros_like(zrecv)
    zrecv2[...] = jnp.zeros_like(zrecv2)

    barrier = pltpu.get_barrier_semaphore()
    for peer in peers:
        pl.semaphore_signal(barrier, inc=1, device_id=peer, device_id_type=MESH)

    def rows(slot):
        return pl.ds(pl.multiple_of(slot * T, T), T)

    own_k = pltpu.make_async_copy(k, kbuf.at[rows(c)], own_sem.at[0])
    own_v = pltpu.make_async_copy(v, vbuf.at[rows(c)], own_sem.at[1])
    loads = [
        pltpu.make_async_copy(src, dst, own_sem.at[2 + i])
        for i, (src, dst) in enumerate(((dt_in, dt), (bc_in, bc), (x_in, x), (q_in, q)))
    ]
    for copy in [own_k, own_v] + loads:
        copy.start()
    pl.semaphore_wait(barrier, len(peers))

    def remote(src, dst, send, recv, peer):
        return pltpu.make_async_remote_copy(
            src_ref=src, dst_ref=dst, send_sem=send, recv_sem=recv,
            device_id=peer, device_id_type=MESH,
        )

    bufs = (kbuf, vbuf)

    def kv_z(step, which):
        return remote(
            (k, v)[which], bufs[which].at[rows(c)], kvz_send.at[step - 1, which],
            kv_recv.at[which, c], at_z(step),
        )

    def kv_y(back, lane, which, slot, step):
        return remote(
            bufs[which].at[rows(slot)], bufs[which].at[rows(slot)], kvy_send.at[back, lane],
            kv_recv.at[which, slot], at_y(step),
        )

    def kv_wait(which, slot):
        remote(
            bufs[which].at[rows(slot)], bufs[which].at[rows(slot)], own_sem.at[which],
            kv_recv.at[which, slot], at_y(1),
        ).wait_recv()

    def y_sends(back):
        slot = (z - back) * ROW + y
        return [
            kv_y(back, 0, 0, slot, 1), kv_y(back, 1, 1, slot, 3),
            kv_y(back, 2, 1, slot, 1), kv_y(back, 3, 0, slot, 3),
        ]

    def slot_of(back, step):
        return (z - back) * ROW + (y + step) % ROW

    def forwards(back):
        return [kv_y(back, 4, 0, slot_of(back, 3), 1), kv_y(back, 5, 1, slot_of(back, 1), 3)]

    for step in (3, 2, 1):

        @pl.when(z + step < ROW)
        def _():
            for which in range(2):
                kv_z(step, which).start()

    own_k.wait()
    own_v.wait()
    for copy in y_sends(0):
        copy.start()

    def pass_down(back):
        for which in range(2):
            kv_wait(which, slot_of(back, 0))
        for copy in y_sends(back):
            copy.start()

    def pass_on(back):
        kv_wait(0, slot_of(back, 3))
        kv_wait(1, slot_of(back, 1))
        for copy in forwards(back):
            copy.start()

    def settle(back):
        kv_wait(1, slot_of(back, 3))
        kv_wait(0, slot_of(back, 1))
        for which in range(2):
            kv_wait(which, slot_of(back, 2))

    def group_cut(part, sub):
        g = 2 * part + sub
        return slice(g * 128, (g + 1) * 128)

    for copy in loads[:3]:
        copy.wait()
    bias = column(dtb)
    rate = jnp.exp(column(alog))
    shifted = dt[...] + bias
    step_size = jnp.maximum(shifted, 0.0) + jnp.log1p(jnp.exp(-jnp.abs(shifted)))
    decay = -step_size * rate
    upto = marks((T, T), lambda s, t: s <= t)
    same = marks((T, T), lambda s, t: s == t)
    cum_t = summed(nn, decay, upto)
    cum_c = summed(nt, cum_t, same, left=False)
    total = cum_t[:, T - 1 : T]
    cumt[...] = cum_t
    stept[...] = step_size
    spread = marks((HG, CH), lambda h, j: (j >> 6) == h)
    tail_step = jnp.exp(total - cum_t) * step_size
    ts_full[...] = summed(tn, tail_step, spread, 2)
    xs[...] = (ts_full[...] * x[...].astype(F32)).astype(BF16)
    pick_b = marks((T, 2 * T), lambda t, r: r == 2 * t)
    pick_c = marks((T, 2 * T), lambda t, r: r == 2 * t + 1)
    b_f = nn(pick_b, bc[...])
    c_f = nn(pick_c, bc[...])
    b_rows = b_f.astype(BF16)
    c_rows = c_f.astype(BF16)
    b_cols = b_f.T.astype(BF16)
    c_cols = c_f.T.astype(BF16)

    tot[pl.ds(c, 1)] = jnp.broadcast_to(
        jnp.concatenate([cum_c[T - 1 : T, :], jnp.zeros((1, 128 - HG), F32)], axis=1)[None],
        (1, 8, 128),
    )
    for sub in range(2):
        for part in range(4):
            ysend[sub, part] = nn(b_cols, xs[:, group_cut(part, sub)]).astype(BF16)

    def tot_y(step):
        return remote(
            tot.at[pl.ds(c, 1)], tot.at[pl.ds(c, 1)], tot_send.at[0, step - 1],
            tot_recv.at[0, y], at_y(step),
        )

    def tot_y_wait(step):
        other = (y + step) % ROW
        remote(
            tot.at[pl.ds(c, 1)], tot.at[pl.ds(z * ROW + other, 1)], tot_send.at[0, step - 1],
            tot_recv.at[0, other], at_y(step),
        ).wait_recv()

    def tot_z(step):
        return remote(
            tot.at[pl.ds(z * ROW, ROW)], tot.at[pl.ds(z * ROW, ROW)], tot_send.at[1, step - 1],
            tot_recv.at[1, z], at_z(step),
        )

    def tot_z_wait(step):
        other = (z + step) % ROW
        remote(
            tot.at[pl.ds(z * ROW, ROW)], tot.at[pl.ds(other * ROW, ROW)], tot_send.at[1, step - 1],
            tot_recv.at[1, other], at_z(step),
        ).wait_recv()

    def trade(phase, sub, src, dst, step):
        to = (y + step) % ROW
        return remote(
            src.at[sub, to], dst.at[sub, y], scan_send.at[phase, sub, step - 1],
            scan_recv.at[phase, sub, y], at_y(step),
        )

    def trade_wait(phase, sub, src, dst, step):
        other = (y + step) % ROW
        remote(
            src.at[sub, other], dst.at[sub, other], scan_send.at[phase, sub, step - 1],
            scan_recv.at[phase, sub, other], at_y(step),
        ).wait_recv()

    def climb(phase, sub, src, dst, step):
        return remote(
            src.at[sub], dst.at[sub, z], scan_send.at[phase, sub, step - 1],
            scan_recv.at[phase, sub, z], at_z(step),
        )

    def climb_wait(phase, sub, src, dst, step):
        other = (z + step) % ROW
        remote(
            src.at[sub], dst.at[sub, other], scan_send.at[phase, sub, step - 1],
            scan_recv.at[phase, sub, other], at_z(step),
        ).wait_recv()

    def trades(phase, sub, src, dst):
        for step in (2, 1, 3):
            trade(phase, sub, src, dst, step).start()
        dst[sub, pl.ds(y, 1)] = src[sub, pl.ds(y, 1)]

    for step in range(1, ROW):
        tot_y(step).start()
    for sub in range(2):
        trades(0, sub, ysend, yrecv)

    wmat[...] = nt(c_rows, b_rows)
    wtmat[...] = nt(b_rows, c_rows)
    step_c = summed(nt, step_size, same, left=False)
    for h in range(HG):
        cumb[:, h * 128 : (h + 1) * 128] = jnp.broadcast_to(cum_c[:, h : h + 1], (T, 128))
        stepb[:, h * 128 : (h + 1) * 128] = jnp.broadcast_to(step_c[:, h : h + 1], (T, 128))
    ecum_full[...] = summed(tn, jnp.exp(cum_t), spread, 2)

    low_half = iota((T, 128), 1) < 64
    zero_pair = jnp.zeros((T, 128), BF16)

    def halves(pair):
        return jnp.where(low_half, pair, zero_pair), jnp.where(low_half, zero_pair, pair)

    def lanes(index, width):
        return pl.ds(pl.multiple_of(index * width, width), width)

    def mix_pair(pair, carry):
        lower = iota((T, T), 0) >= iota((T, T), 1)
        upper = iota((T, T), 0) <= iota((T, T), 1)
        parts = halves(x[:, lanes(pair, 128)])
        result = jnp.zeros((T, 128), F32)
        for i in range(2):
            h = 2 * pair + i
            at_t = cumb[:, lanes(h, 128)]
            at_t = jnp.concatenate([at_t, at_t], axis=1)
            size_c = stepb[:, lanes(h, 128)]
            size_c = jnp.concatenate([size_c, size_c], axis=1)
            at_s = cumt[pl.ds(h, 1), :]
            size_r = stept[pl.ds(h, 1), :]
            held = jnp.exp(jnp.where(lower, at_t - at_s, NEGATIVE)) * size_r
            timed[h] = held
            mixed = (held * wmat[...]).astype(BF16)
            result = result + nn(mixed, parts[i])
            turned = jnp.exp(jnp.where(upper, at_s - at_t, NEGATIVE)) * size_c
            mixt[h] = (turned * wtmat[...]).astype(BF16)
        intra[:, lanes(pair, 128)] = result
        return carry

    lax.fori_loop(0, GROUP // 2, mix_pair, 0)
    pass_on(0)

    @pl.when(z >= 1)
    def _():
        pass_down(1)

    for step in range(1, ROW):
        tot_y_wait(step)
    for step in range(1, ROW):
        tot_z(step).start()
    lax.fori_loop(GROUP // 2, GROUP, mix_pair, 0)

    tot_all_ready = [tot_z_wait(step) for step in range(1, ROW)]
    del tot_all_ready
    totals = jnp.sum(jnp.where(iota((16, 8, 128), 1) == 0, tot[...], 0.0), axis=1)
    mine = marks((128, QW), lambda h, j: h == y * 4 + (j >> 6))
    here = summed(nn, totals, mine)
    for sub in range(2):
        tq[sub] = here[:, sub * 128 : (sub + 1) * 128]

    def total_of(sub, zz, kk):
        return tq[sub, pl.ds(zz * ROW + kk, 1), :]

    def row_total(sub, zz):
        return sum(total_of(sub, zz, kk) for kk in range(1, ROW)) + total_of(sub, zz, 0)

    def scan_row(phase, sub, src, got, up, pre, order):
        for step in range(1, ROW):
            trade_wait(phase, sub, src, got, step)
        run = jnp.zeros((N, 128), F32)
        for kk in order:
            pre[sub, kk] = run
            run = jnp.exp(total_of(sub, z, kk)) * run + got[sub, kk].astype(F32)
        up[sub] = run.astype(BF16)

    def scan_back(phase, sub, got, back, final, pre, order, rows_in, arrived):
        held = jnp.zeros((N, 128), F32)
        for zz in rows_in:
            held = jnp.where(
                arrived(zz), jnp.exp(row_total(sub, zz)) * held + got[sub, zz].astype(F32), held
            )
        passed = jnp.zeros((1, 128), F32)
        for kk in order:
            back[sub, kk] = (jnp.exp(passed) * held + pre[sub, kk]).astype(BF16)
            passed = passed + total_of(sub, z, kk)
        trades(phase, sub, back, final)

    ahead = (0, 1, 2, 3)
    behind = (3, 2, 1, 0)
    for sub in range(2):
        scan_row(0, sub, ysend, yrecv, zsend, before, ahead)
        for step in range(1, ROW):

            @pl.when(z + step < ROW)
            def _():
                climb(1, sub, zsend, zrecv, step).start()

    ones = jnp.ones((ROW * T, HD), BF16)

    def attend(row, first, heads):
        base = pl.multiple_of(row * (ROW * T), ROW * T)
        start, stride, count = heads

        def one(i, carry):
            g = start + stride * i
            keys = kbuf[pl.ds(base, ROW * T), :]
            both = jnp.concatenate([vbuf[pl.ds(base, ROW * T), :], ones], axis=1)
            scores = nt(q[:, lanes(g, HD)], keys)
            if first:
                seen = iota((T, ROW * T), 1) <= iota((T, ROW * T), 0) + y * T
                scores = jnp.where(seen, scores, NEGATIVE)
            top = jnp.max(scores, axis=1, keepdims=True)
            if first:
                new = jnp.broadcast_to(top, (T, HD))
            else:
                old = m_ref[g]
                new = jnp.maximum(old, top)
            weights = jnp.exp2((scores - jnp.concatenate([new] * 8, axis=1)) * EXP_SCALE)
            part = nn(weights.astype(BF16), both)
            if first:
                acc[g] = part
            else:
                scale = jnp.exp2((old - new) * EXP_SCALE)
                acc[g] = acc[g] * jnp.concatenate([scale, scale], axis=1) + part
            m_ref[g] = new
            return carry

        lax.fori_loop(0, count, one, 0, unroll=4)

    all_heads = (0, 1, GROUP)
    loads[3].wait()
    settle(0)
    attend(z, True, (0, 2, GROUP // 2))

    @pl.when(z >= 2)
    def _():
        pass_down(2)

    @pl.when(z >= 1)
    def _():
        pass_on(1)

    @pl.when(z >= 3)
    def _():
        pass_down(3)

    attend(z, True, (1, 2, GROUP // 2))

    @pl.when(z >= 2)
    def _():
        pass_on(2)

    for sub in range(2):
        for step in range(1, ROW):

            @pl.when(z >= step)
            def _():
                climb_wait(1, sub, zsend, zrecv, ROW - step)

        scan_back(2, sub, zrecv, bsend, brecv, before, ahead, (0, 1, 2), lambda zz: zz < z)

    @pl.when(z >= 2)
    def _():
        settle(1)
        attend(z - 1, False, all_heads)

    @pl.when(z >= 3)
    def _():
        pass_on(3)
        settle(2)
        attend(z - 2, False, all_heads)

    for sub in range(2):
        for step in range(1, ROW):
            trade_wait(2, sub, bsend, brecv, step)
        for part in range(4):
            cut = group_cut(part, sub)
            inter[:, cut] = ecum_full[:, cut] * nn(c_rows, brecv[sub, part])

    @pl.when(z >= 1)
    def _():
        settle(z)

    skip_row = summed(nn, jnp.broadcast_to(skp[...], (8, HG)), spread)[0:1, :]

    def fold(a):
        a = a.reshape(T // 8, 8, a.shape[1])
        a = jnp.sum(a, axis=0)
        out = a[:, 0:128]
        for j in range(1, a.shape[1] // 128):
            out = out + a[:, j * 128 : (j + 1) * 128]
        return out

    power = jnp.zeros((8, 128), F32)
    error = jnp.zeros((8, 128), F32)
    for sub in range(2):

        @pl.when(z >= 1)
        def _():
            attend(0, False, (sub, 2, GROUP // 2))

        for part in range(4):
            cut = group_cut(part, sub)
            both = acc[2 * part + sub]
            goal = (both[:, :HD] / both[:, HD:]).astype(BF16).astype(F32)
            made = intra[:, cut] + inter[:, cut] + skip_row[:, cut] * x[:, cut].astype(F32)
            resid = made - goal
            power = power + fold(goal * goal)
            error = error + fold(resid * resid)
            up = 2.0 * resid
            ups[:, cut] = up
            upb[:, cut] = up.astype(BF16)
            eu[:, cut] = (ecum_full[:, cut] * up).astype(BF16)
            ysend2[sub, part] = nn(c_cols, eu[:, cut]).astype(BF16)
        trades(3, sub, ysend2, yrecv2)

    def spread_out(buf, place, stage, at, size):
        out = []
        for step in range(1, size):
            out.append(
                remote(
                    buf.at[pl.ds(place, 1)], buf.at[pl.ds(place, 1)], red_send.at[stage, step - 1],
                    red_recv.at[stage, place], at(step),
                )
            )
        return out

    def collect(buf, place, stage, at, size):
        for step in range(1, size):
            other = (place + step) % size
            remote(
                buf.at[pl.ds(place, 1)], buf.at[pl.ds(other, 1)], red_send.at[stage, step - 1],
                red_recv.at[stage, other], at(step),
            ).wait_recv()
        total = buf[0]
        for j in range(1, size):
            total = total + buf[j]
        return total

    def launch(value, buf, place, stage, at, size):
        buf[pl.ds(place, 1)] = value[None]
        for copy in spread_out(buf, place, stage, at, size):
            copy.start()

    launch(jnp.concatenate([power, error], axis=0), sy, y, 0, at_y, ROW)

    for sub in range(2):
        scan_row(3, sub, ysend2, yrecv2, zsend2, before, behind)
        for step in range(1, ROW):

            @pl.when(z >= step)
            def _():
                climb(4, sub, zsend2, zrecv2, ROW - step).start()

    launch(collect(sy, y, 0, at_y, ROW), sz, z, 1, at_z, ROW)

    def pair_products(pair, running):
        ups_pair = halves(upb[:, lanes(pair, 128)])
        x_pair = x[:, lanes(pair, 128)]
        through = jnp.zeros((T, 128), F32)
        for i in range(2):
            h = 2 * pair + i
            running = running + timed[h] * nt(ups_pair[i], x_pair)
            through = through + nn(mixt[h], ups_pair[i])
        t1[:, lanes(pair, 128)] = through
        return running

    paired = lax.fori_loop(0, GROUP // 2, pair_products, jnp.zeros((T, T), F32))
    launch(collect(sz, z, 1, at_z, ROW), sd, d, 2, at_d, dp_size)
    paired = lax.fori_loop(GROUP // 2, GROUP, pair_products, paired)
    for sub in range(2):
        for step in range(1, ROW):

            @pl.when(z + step < ROW)
            def _():
                climb_wait(4, sub, zsend2, zrecv2, step)

        scan_back(5, sub, zrecv2, bsend2, brecv2, before, behind, (3, 2, 1), lambda zz: zz > z)
    launch(collect(sd, d, 2, at_d, dp_size), st, tt, 3, at_t, tensor_size)

    paired_rows = paired.astype(BF16)
    paired_cols = paired.T.astype(BF16)
    grad_b = nn(paired_cols, c_rows)
    grad_c = nn(paired_rows, b_rows)
    for sub in range(2):
        for part in range(4):
            grad_c = grad_c + nt(eu[:, group_cut(part, sub)], brecv[sub, part])

    def by_head(a):
        return summed(nt, a, spread, 2, left=False)

    heads_at = marks((CH, 128), lambda j, h: (j >> 6) == h)
    heads_next = marks((CH, 128), lambda j, h: (j >> 6) == h - HG)
    xf = x[...].astype(F32)
    through_x = xf * t1[...]
    gains = upb[...].astype(F32) * intra[...] - through_x + ups[...] * inter[...]
    stats = summed(nn, gains, heads_at, 2) + nn(through_x.astype(BF16), heads_next)
    stats = stats.T
    gained = stats[0:HG]
    from_mix = stats[HG : 2 * HG]
    skip_part = jnp.sum((ups[...] * xf).reshape(T // 8, 8, CH), axis=0)
    skip_term = jnp.sum(by_head(skip_part), axis=1, keepdims=True)
    since = marks((T, T), lambda s, t: s >= t)
    until = marks((T, T), lambda s, t: s < t)
    gained_after = summed(nn, gained, since)
    gate = 1.0 / (1.0 + jnp.exp(-shifted))

    both_sums = collect(st, tt, 3, at_t, tensor_size)
    power_all = jnp.sum(both_sums[0:8, :], keepdims=True)
    error_all = jnp.sum(both_sums[8:16, :], keepdims=True)
    mean_square = power_all / entries + EPSILON
    factor = 1.0 / mean_square
    gls[...] = jnp.broadcast_to(error_all / mean_square / entries, (8, 128))

    overlap = [None] * 8
    later_stats = jnp.zeros((T, 128), F32)
    for sub in range(2):
        for step in range(1, ROW):
            trade_wait(5, sub, bsend2, brecv2, step)
        for part in range(4):
            cut = group_cut(part, sub)
            later = brecv2[sub, part]
            came = ts_full[:, cut] * nn(b_rows, later)
            inter[:, cut] = came
            later_stats = later_stats + nn(
                (x[:, cut].astype(F32) * came).astype(BF16), heads_at[cut, :]
            )
            prod = later.astype(F32) * brecv[sub, part].astype(F32)
            overlap[2 * part + sub] = jnp.sum(prod.reshape(N // 8, 8, 128), axis=0)
    from_later = later_stats.T[0:HG]
    meet = jnp.sum(by_head(jnp.concatenate(overlap, axis=1)), axis=1, keepdims=True)
    decay_grad = gained_after + summed(nn, from_later, until) + jnp.exp(total) * meet
    direct = (from_mix + from_later) / step_size
    shift_grad = (direct - decay_grad * rate) * gate
    decay_term = jnp.sum(decay_grad * decay, axis=1, keepdims=True)
    shift_term = jnp.sum(shift_grad, axis=1, keepdims=True)
    lane = iota((HG, 128), 1)
    heads = jnp.where(lane == 0, decay_term, jnp.where(lane == 1, shift_term, skip_term))
    launch(heads, hy, y, 4, at_y, ROW)
    gdt[...] = shift_grad * factor
    for sub in range(2):
        for part in range(4):
            grad_b = grad_b + nt(xs[:, group_cut(part, sub)], brecv2[sub, part])
    launch(collect(hy, y, 4, at_y, ROW), hz, z, 5, at_z, ROW)
    put_b = marks((2 * T, T), lambda r, t: r == 2 * t)
    put_c = marks((2 * T, T), lambda r, t: r == 2 * t + 1)
    gbc[...] = (
        nn(put_b, (grad_b * factor).astype(BF16)) + nn(put_c, (grad_c * factor).astype(BF16))
    ).astype(BF16)
    launch(collect(hz, z, 5, at_z, ROW), hd, d, 6, at_d, dp_size)
    gx[...] = ((skip_row * ups[...] + t1[...] + inter[...]) * factor).astype(BF16)
    ghd[...] = collect(hd, d, 6, at_d, dp_size) * factor

    for step in range(1, ROW):

        @pl.when(z + step < ROW)
        def _():
            for which in range(2):
                kv_z(step, which).wait_send()
            for sub in range(2):
                climb(1, sub, zsend, zrecv, step).wait_send()

        @pl.when(z >= step)
        def _():
            for sub in range(2):
                climb(4, sub, zsend2, zrecv2, ROW - step).wait_send()

        tot_y(step).wait_send()
        tot_z(step).wait_send()
        for sub in range(2):
            trade(0, sub, ysend, yrecv, step).wait_send()
            trade(2, sub, bsend, brecv, step).wait_send()
            trade(3, sub, ysend2, yrecv2, step).wait_send()
            trade(5, sub, bsend2, brecv2, step).wait_send()
    for back in range(ROW):

        @pl.when(z >= back)
        def _():
            for copy in y_sends(back) + forwards(back):
                copy.wait_send()

    for buf, place, stage, at, size in (
        (sy, y, 0, at_y, ROW), (sz, z, 1, at_z, ROW), (sd, d, 2, at_d, dp_size),
        (st, tt, 3, at_t, tensor_size), (hy, y, 4, at_y, ROW), (hz, z, 5, at_z, ROW),
        (hd, d, 6, at_d, dp_size),
    ):
        for copy in spread_out(buf, place, stage, at, size):
            copy.wait_send()


def write_out(gx, gbc, gdt, ghd, gls, ogx, ogbc, ogdt, oghd, ogls):
    ogx[...] = gx[...]
    ogbc[...] = gbc[...]
    ogdt[...] = gdt[...]
    turned = ghd[...].T
    for i in range(3):
        oghd[i] = turned[i : i + 1, :]
    ogls[...] = gls[0:1, 0:1]


def solution(mesh):
    dp_size, tensor_size = mesh.shape["dp"], mesh.shape["tensor"]
    entries = float(dp_size * mesh.shape["ctx"] * tensor_size * T * CH)

    def vm(shape, kind):
        return pltpu.VMEM(shape, kind)

    chunk4 = (2, ROW, N, 128)
    scratch = [
        vm((T, CH), BF16), vm((T, CH), BF16), vm((2 * T, N), BF16), vm((HG, T), F32),
        vm((16 * T, HD), BF16), vm((16 * T, HD), BF16),
        vm((GROUP, T, HD), F32), vm((GROUP, T, 2 * HD), F32),
        vm((HG, T, T), F32), vm((HG, T, T), BF16),
        vm((T, HG * 128), F32), vm((T, HG * 128), F32),
        vm((HG, T), F32), vm((HG, T), F32), vm((T, T), F32), vm((T, T), F32),
        vm((T, CH), F32), vm((T, CH), F32), vm((T, CH), BF16), vm((T, CH), F32),
        vm((T, CH), F32), vm((T, CH), F32), vm((T, CH), BF16), vm((T, CH), BF16),
        vm((T, CH), F32),
        vm((16, 8, 128), F32), vm((2, 16, 128), F32), vm((2, ROW, N, 128), F32),
    ]
    for _ in range(2):
        scratch += [
            vm(chunk4, BF16), vm(chunk4, BF16), vm((2, N, 128), BF16), vm(chunk4, BF16),
            vm(chunk4, BF16), vm(chunk4, BF16),
        ]
    scratch += [
        vm((ROW, 16, 128), F32), vm((ROW, 16, 128), F32), vm((dp_size, 16, 128), F32),
        vm((tensor_size, 16, 128), F32), vm((ROW, 16, 128), F32), vm((ROW, 16, 128), F32),
        vm((dp_size, 16, 128), F32),
    ]
    sem = pltpu.SemaphoreType.DMA
    scratch += [
        sem((6,)), sem((2, 16)), sem((3, 2)), sem((4, 6)),
        sem((2, 3)), sem((2, 4)), sem((6, 2, 3)), sem((6, 2, 4)), sem((7, 3)), sem((7, 4)),
    ]

    def body(queries, keys, values, student_x, student_bc, student_dt, a_log, dt_bias, skip):
        whole = pl.BlockSpec(memory_space=pltpu.VMEM)
        far = pl.BlockSpec(memory_space=pltpu.HBM)

        def run(*refs):
            kernel(entries, dp_size, tensor_size, *refs)

        gx, gbc, gdt, ghd, gls = pl.pallas_call(
            run,
            out_shape=(
                jax.ShapeDtypeStruct((T, CH), BF16),
                jax.ShapeDtypeStruct((2 * T, N), BF16),
                jax.ShapeDtypeStruct((HG, T), F32),
                jax.ShapeDtypeStruct((HG, 128), F32),
                jax.ShapeDtypeStruct((8, 128), F32),
            ),
            in_specs=[far] * 6 + [whole] * 3,
            out_specs=(whole,) * 5,
            scratch_shapes=scratch,
            compiler_params=pltpu.CompilerParams(
                collective_id=0, has_side_effects=True, vmem_limit_bytes=61 * 1024 * 1024
            ),
            name="align",
        )(
            queries.reshape(T, CH), keys.reshape(T, HD), values.reshape(T, HD),
            student_x.reshape(T, CH), student_bc.reshape(2 * T, N),
            student_dt.reshape(T, HG).T, a_log, dt_bias, skip,
        )
        gx, gbc, gdt, ghd, gls = pl.pallas_call(
            write_out,
            out_shape=(
                jax.ShapeDtypeStruct((T, CH), BF16),
                jax.ShapeDtypeStruct((2 * T, N), BF16),
                jax.ShapeDtypeStruct((HG, T), F32),
                jax.ShapeDtypeStruct((3, 1, HG), F32),
                jax.ShapeDtypeStruct((1, 1), F32),
            ),
            in_specs=[whole] * 5,
            out_specs=(whole,) * 5,
            compiler_params=pltpu.CompilerParams(vmem_limit_bytes=61 * 1024 * 1024),
            name="write_out",
        )(gx, gbc, gdt, ghd, gls)
        return (
            gx.reshape(1, T, 1, CH),
            gbc.reshape(1, T, 1, 2, N),
            gdt.T.reshape(1, T, 1, HG),
            ghd,
            gls.reshape(()),
        )

    return jax.shard_map(
        body,
        mesh=mesh,
        in_specs=(
            P("dp", "ctx", "tensor", None),
            P("dp", "ctx", "tensor", None),
            P("dp", "ctx", "tensor", None),
            P("dp", "ctx", "tensor", None),
            P("dp", "ctx", "tensor", None, None),
            P("dp", "ctx", "tensor", None),
            P("tensor", None),
            P("tensor", None),
            P("tensor", None),
        ),
        out_specs=(
            P("dp", "ctx", "tensor", None),
            P("dp", "ctx", "tensor", None, None),
            P("dp", "ctx", "tensor", None),
            P(None, "tensor", None),
            P(),
        ),
        check_vma=False,
    )
```

```python
import jax
import jax.numpy as jnp
from jax import lax
from jax.experimental import pallas as pl
from jax.experimental.pallas import tpu as pltpu
from jax.sharding import PartitionSpec as P

T = 256
HD = 128
GROUP = 8
N = 128
HG = 16
CH = 1024
QW = 256
ROW = 4
F32 = jnp.float32
BF16 = jnp.bfloat16
NEGATIVE = -1e30
EPSILON = 1e-06
EXP_SCALE = 1.4426950408889634 * HD**-0.5
MESH = pl.DeviceIdType.MESH


def nn(a, b):
    return lax.dot_general(a, b, (((1,), (0,)), ((), ())), preferred_element_type=F32)


def nt(a, b):
    return lax.dot_general(a, b, (((1,), (1,)), ((), ())), preferred_element_type=F32)


def tn(a, b):
    return lax.dot_general(a, b, (((0,), (0,)), ((), ())), preferred_element_type=F32)


def pieces(a, count):
    out = []
    for _ in range(count - 1):
        top = a.astype(BF16)
        out.append(top)
        a = a - top.astype(F32)
    out.append(a.astype(BF16))
    return out


def summed(form, values, marks, count=3, left=True):
    total = None
    for part in pieces(values, count):
        term = form(part, marks) if left else form(marks, part)
        total = term if total is None else total + term
    return total


def iota(shape, dim):
    return lax.broadcasted_iota(jnp.int32, shape, dim)


def marks(shape, test):
    return jnp.where(test(iota(shape, 0), iota(shape, 1)), 1.0, 0.0).astype(BF16)


def column(ref):
    wide = jnp.broadcast_to(ref[...], (HG, HG))
    same = iota((HG, HG), 0) == iota((HG, HG), 1)
    return jnp.sum(jnp.where(same, wide, 0.0), axis=1, keepdims=True)


def kernel(
    entries, dp_size, tensor_size,
    q_in, k, v, x_in, bc_in, dt_in, alog, dtb, skp,
    gx, gbc, gdt, ghd, gls,
    q, x, bc, dt, kbuf, vbuf, m_ref, acc, timed, mixt, cumb, stepb, cumt, stept, wmat, wtmat,
    intra, inter, upb, ups, ts_full, ecum_full, xs, eu, t1,
    tot, tq, gq, before, weight_z, weight_y, eu_like, zysend, zyrecv,
    ysend, yrecv, zsend, zrecv, bsend, brecv,
    ysend2, yrecv2, zsend2, zrecv2, bsend2, brecv2,
    sy, sz, sd, st, hy, hz, hd,
    own_sem, kv_recv, kvz_send, kvy_send,
    tot_send, tot_recv, scan_send, scan_recv, red_send, red_recv, zy_send, zy_recv,
):
    c = lax.axis_index("ctx")
    d = lax.axis_index("dp")
    tt = lax.axis_index("tensor")
    z = c // ROW
    y = c % ROW

    def at_y(step):
        return {"ctx": z * ROW + (y + step) % ROW}

    def at_z(step):
        return {"ctx": ((z + step) % ROW) * ROW + y}

    def at_d(step):
        return {"dp": (d + step) % dp_size}

    def at_t(step):
        return {"tensor": (tt + step) % tensor_size}

    peers = [at_y(s) for s in range(1, ROW)] + [at_z(s) for s in range(1, ROW)]
    peers += [at_d(s) for s in range(1, dp_size)] + [at_t(s) for s in range(1, tensor_size)]

    zrecv[...] = jnp.zeros_like(zrecv)
    zrecv2[...] = jnp.zeros_like(zrecv2)

    barrier = pltpu.get_barrier_semaphore()
    for peer in peers:
        pl.semaphore_signal(barrier, inc=1, device_id=peer, device_id_type=MESH)

    def rows(slot):
        return pl.ds(pl.multiple_of(slot * T, T), T)

    own_k = pltpu.make_async_copy(k, kbuf.at[rows(c)], own_sem.at[0])
    own_v = pltpu.make_async_copy(v, vbuf.at[rows(c)], own_sem.at[1])
    loads = [
        pltpu.make_async_copy(src, dst, own_sem.at[2 + i])
        for i, (src, dst) in enumerate(((dt_in, dt), (bc_in, bc), (x_in, x), (q_in, q)))
    ]
    for copy in [own_k, own_v] + loads:
        copy.start()
    pl.semaphore_wait(barrier, len(peers))

    def remote(src, dst, send, recv, peer):
        return pltpu.make_async_remote_copy(
            src_ref=src, dst_ref=dst, send_sem=send, recv_sem=recv,
            device_id=peer, device_id_type=MESH,
        )

    bufs = (kbuf, vbuf)

    def kv_z(step, which):
        return remote(
            (k, v)[which], bufs[which].at[rows(c)], kvz_send.at[step - 1, which],
            kv_recv.at[which, c], at_z(step),
        )

    def kv_y(back, lane, which, slot, step):
        return remote(
            bufs[which].at[rows(slot)], bufs[which].at[rows(slot)], kvy_send.at[back, lane],
            kv_recv.at[which, slot], at_y(step),
        )

    def kv_wait(which, slot):
        remote(
            bufs[which].at[rows(slot)], bufs[which].at[rows(slot)], own_sem.at[which],
            kv_recv.at[which, slot], at_y(1),
        ).wait_recv()

    def y_sends(back):
        slot = (z - back) * ROW + y
        return [
            kv_y(back, 0, 0, slot, 1), kv_y(back, 1, 1, slot, 3),
            kv_y(back, 2, 1, slot, 1), kv_y(back, 3, 0, slot, 3),
        ]

    def slot_of(back, step):
        return (z - back) * ROW + (y + step) % ROW

    def forwards(back):
        return [kv_y(back, 4, 0, slot_of(back, 3), 1), kv_y(back, 5, 1, slot_of(back, 1), 3)]

    for step in (3, 2, 1):

        @pl.when(z + step < ROW)
        def _():
            for which in range(2):
                kv_z(step, which).start()

    own_k.wait()
    own_v.wait()
    for copy in y_sends(0):
        copy.start()

    def pass_down(back):
        for which in range(2):
            kv_wait(which, slot_of(back, 0))
        for copy in y_sends(back):
            copy.start()

    def pass_on(back):
        kv_wait(0, slot_of(back, 3))
        kv_wait(1, slot_of(back, 1))
        for copy in forwards(back):
            copy.start()

    def settle(back):
        kv_wait(1, slot_of(back, 3))
        kv_wait(0, slot_of(back, 1))
        for which in range(2):
            kv_wait(which, slot_of(back, 2))

    def group_cut(part, sub):
        g = 2 * part + sub
        return slice(g * 128, (g + 1) * 128)

    for copy in loads[:3]:
        copy.wait()
    bias = column(dtb)
    rate = jnp.exp(column(alog))
    shifted = dt[...] + bias
    step_size = jnp.maximum(shifted, 0.0) + jnp.log1p(jnp.exp(-jnp.abs(shifted)))
    decay = -step_size * rate
    upto = marks((T, T), lambda s, t: s <= t)
    same = marks((T, T), lambda s, t: s == t)
    cum_t = summed(nn, decay, upto)
    cum_c = summed(nt, cum_t, same, left=False)
    total = cum_t[:, T - 1 : T]
    cumt[...] = cum_t
    stept[...] = step_size
    spread = marks((HG, CH), lambda h, j: (j >> 6) == h)
    tail_step = jnp.exp(total - cum_t) * step_size
    ts_full[...] = summed(tn, tail_step, spread, 2)
    xs[...] = (ts_full[...] * x[...].astype(F32)).astype(BF16)
    pick_b = marks((T, 2 * T), lambda t, r: r == 2 * t)
    pick_c = marks((T, 2 * T), lambda t, r: r == 2 * t + 1)
    b_f = nn(pick_b, bc[...])
    c_f = nn(pick_c, bc[...])
    b_rows = b_f.astype(BF16)
    c_rows = c_f.astype(BF16)
    b_cols = b_f.T.astype(BF16)
    c_cols = c_f.T.astype(BF16)

    gate = 1.0 / (1.0 + jnp.exp(-shifted))
    later_than = marks((T, T), lambda s, t: s > t)
    gate_after = summed(nn, gate, later_than)
    gate_sum = jnp.broadcast_to(jnp.sum(gate, axis=1, keepdims=True) * rate, (HG, 128))
    gate_row = jnp.sum(
        jnp.where(iota((HG, 128), 1) == iota((HG, 128), 0) + HG, gate_sum, 0.0),
        axis=0, keepdims=True,
    )
    total_row = jnp.sum(
        jnp.where(
            iota((HG, 128), 1) == iota((HG, 128), 0), jnp.broadcast_to(total, (HG, 128)), 0.0
        ),
        axis=0, keepdims=True,
    )
    tot[pl.ds(c, 1)] = jnp.broadcast_to((total_row + gate_row)[None], (1, 8, 128))
    weight_z[...] = tail_step * (total - cum_t)
    weight_y[...] = tail_step * (gate / step_size - rate * gate_after)
    for sub in range(2):
        for part in range(4):
            ysend[sub, part] = nn(b_cols, xs[:, group_cut(part, sub)]).astype(BF16)

    def tot_y(step):
        return remote(
            tot.at[pl.ds(c, 1)], tot.at[pl.ds(c, 1)], tot_send.at[0, step - 1],
            tot_recv.at[0, y], at_y(step),
        )

    def tot_y_wait(step):
        other = (y + step) % ROW
        remote(
            tot.at[pl.ds(c, 1)], tot.at[pl.ds(z * ROW + other, 1)], tot_send.at[0, step - 1],
            tot_recv.at[0, other], at_y(step),
        ).wait_recv()

    def tot_z(step):
        return remote(
            tot.at[pl.ds(z * ROW, ROW)], tot.at[pl.ds(z * ROW, ROW)], tot_send.at[1, step - 1],
            tot_recv.at[1, z], at_z(step),
        )

    def tot_z_wait(step):
        other = (z + step) % ROW
        remote(
            tot.at[pl.ds(z * ROW, ROW)], tot.at[pl.ds(other * ROW, ROW)], tot_send.at[1, step - 1],
            tot_recv.at[1, other], at_z(step),
        ).wait_recv()

    def trade(phase, sub, src, dst, step):
        to = (y + step) % ROW
        return remote(
            src.at[sub, to], dst.at[sub, y], scan_send.at[phase, sub, step - 1],
            scan_recv.at[phase, sub, y], at_y(step),
        )

    def trade_wait(phase, sub, src, dst, step):
        other = (y + step) % ROW
        remote(
            src.at[sub, other], dst.at[sub, other], scan_send.at[phase, sub, step - 1],
            scan_recv.at[phase, sub, other], at_y(step),
        ).wait_recv()

    def climb(phase, sub, src, dst, step):
        return remote(
            src.at[sub], dst.at[sub, z], scan_send.at[phase, sub, step - 1],
            scan_recv.at[phase, sub, z], at_z(step),
        )

    def climb_wait(phase, sub, src, dst, step):
        other = (z + step) % ROW
        remote(
            src.at[sub], dst.at[sub, other], scan_send.at[phase, sub, step - 1],
            scan_recv.at[phase, sub, other], at_z(step),
        ).wait_recv()

    def trades(phase, sub, src, dst):
        for step in (2, 1, 3):
            trade(phase, sub, src, dst, step).start()
        dst[sub, pl.ds(y, 1)] = src[sub, pl.ds(y, 1)]

    for step in range(1, ROW):
        tot_y(step).start()
    for sub in range(2):
        trades(0, sub, ysend, yrecv)

    wmat[...] = nt(c_rows, b_rows)
    wtmat[...] = nt(b_rows, c_rows)
    step_c = summed(nt, step_size, same, left=False)
    for h in range(HG):
        cumb[:, h * 128 : (h + 1) * 128] = jnp.broadcast_to(cum_c[:, h : h + 1], (T, 128))
        stepb[:, h * 128 : (h + 1) * 128] = jnp.broadcast_to(step_c[:, h : h + 1], (T, 128))
    ecum_full[...] = summed(tn, jnp.exp(cum_t), spread, 2)

    low_half = iota((T, 128), 1) < 64
    zero_pair = jnp.zeros((T, 128), BF16)

    def halves(pair):
        return jnp.where(low_half, pair, zero_pair), jnp.where(low_half, zero_pair, pair)

    def lanes(index, width):
        return pl.ds(pl.multiple_of(index * width, width), width)

    def mix_pair(pair, carry):
        lower = iota((T, T), 0) >= iota((T, T), 1)
        upper = iota((T, T), 0) <= iota((T, T), 1)
        parts = halves(x[:, lanes(pair, 128)])
        result = jnp.zeros((T, 128), F32)
        for i in range(2):
            h = 2 * pair + i
            at_t = cumb[:, lanes(h, 128)]
            at_t = jnp.concatenate([at_t, at_t], axis=1)
            size_c = stepb[:, lanes(h, 128)]
            size_c = jnp.concatenate([size_c, size_c], axis=1)
            at_s = cumt[pl.ds(h, 1), :]
            size_r = stept[pl.ds(h, 1), :]
            held = jnp.exp(jnp.where(lower, at_t - at_s, NEGATIVE)) * size_r
            timed[h] = held
            mixed = (held * wmat[...]).astype(BF16)
            result = result + nn(mixed, parts[i])
            turned = jnp.exp(jnp.where(upper, at_s - at_t, NEGATIVE)) * size_c
            mixt[h] = (turned * wtmat[...]).astype(BF16)
        intra[:, lanes(pair, 128)] = result
        return carry


    @pl.when(z >= 1)
    def _():
        pass_down(1)

    pass_on(0)
    lax.fori_loop(0, GROUP // 2, mix_pair, 0)
    for step in range(1, ROW):
        tot_y_wait(step)
    for step in range(1, ROW):
        tot_z(step).start()
    lax.fori_loop(GROUP // 2, GROUP, mix_pair, 0)

    tot_all_ready = [tot_z_wait(step) for step in range(1, ROW)]
    del tot_all_ready
    totals = jnp.sum(jnp.where(iota((16, 8, 128), 1) == 0, tot[...], 0.0), axis=1)
    mine = marks((128, QW), lambda h, j: h == y * 4 + (j >> 6))
    mine_next = marks((128, QW), lambda h, j: h == HG + y * 4 + (j >> 6))
    here = summed(nn, totals, mine)
    here_next = summed(nn, totals, mine_next)
    for sub in range(2):
        tq[sub] = here[:, sub * 128 : (sub + 1) * 128]
        gq[sub] = here_next[:, sub * 128 : (sub + 1) * 128]

    def total_of(sub, zz, kk):
        return tq[sub, pl.ds(zz * ROW + kk, 1), :]

    def row_total(sub, zz):
        return sum(total_of(sub, zz, kk) for kk in range(1, ROW)) + total_of(sub, zz, 0)

    def scan_row(phase, sub, src, got, up, pre, order):
        for step in range(1, ROW):
            trade_wait(phase, sub, src, got, step)
        run = jnp.zeros((N, 128), F32)
        for kk in order:
            pre[sub, kk] = run
            run = jnp.exp(total_of(sub, z, kk)) * run + got[sub, kk].astype(F32)
        up[sub] = run.astype(BF16)

    def scan_back(phase, sub, got, back, final, pre, order, rows_in, arrived):
        held = jnp.zeros((N, 128), F32)
        for zz in rows_in:
            held = jnp.where(
                arrived(zz), jnp.exp(row_total(sub, zz)) * held + got[sub, zz].astype(F32), held
            )
        passed = jnp.zeros((1, 128), F32)
        for kk in order:
            back[sub, kk] = (jnp.exp(passed) * held + pre[sub, kk]).astype(BF16)
            passed = passed + total_of(sub, z, kk)
        trades(phase, sub, back, final)

    def tiles(a):
        return jnp.sum(a.reshape(N // 8, 8, 128), axis=0)

    def functionals(sub):
        for_decay = jnp.zeros((8, 128), F32)
        for_shift = jnp.zeros((8, 128), F32)
        for kk in range(ROW):
            later = bsend2[sub, kk].astype(F32)
            sofar = total_of(sub, z, kk)
            met = jnp.exp(sofar) * tiles(later * bsend[sub, kk].astype(F32))
            gates = gq[sub, pl.ds(z * ROW + kk, 1), :]
            for_decay = for_decay + tiles(later * zyrecv[kk, 2 * sub].astype(F32)) + sofar * met
            for_shift = for_shift + tiles(later * zyrecv[kk, 2 * sub + 1].astype(F32)) - gates * met
        return for_decay, for_shift

    ahead = (0, 1, 2, 3)
    behind = (3, 2, 1, 0)
    for sub in range(2):
        scan_row(0, sub, ysend, yrecv, zsend, before, ahead)
        for step in range(1, ROW):

            @pl.when(z + step < ROW)
            def _():
                climb(1, sub, zsend, zrecv, step).start()

    ones = jnp.ones((ROW * T, HD), BF16)

    def attend(row, first, heads):
        base = pl.multiple_of(row * (ROW * T), ROW * T)
        start, stride, count = heads

        def one(i, carry):
            g = start + stride * i
            keys = kbuf[pl.ds(base, ROW * T), :]
            both = jnp.concatenate([vbuf[pl.ds(base, ROW * T), :], ones], axis=1)
            scores = nt(q[:, lanes(g, HD)], keys)
            if first:
                seen = iota((T, ROW * T), 1) <= iota((T, ROW * T), 0) + y * T
                scores = jnp.where(seen, scores, NEGATIVE)
            top = jnp.max(scores, axis=1, keepdims=True)
            if first:
                new = jnp.broadcast_to(top, (T, HD))
            else:
                old = m_ref[g]
                new = jnp.maximum(old, top)
            weights = jnp.exp2((scores - jnp.concatenate([new] * 8, axis=1)) * EXP_SCALE)
            part = nn(weights.astype(BF16), both)
            if first:
                acc[g] = part
            else:
                scale = jnp.exp2((old - new) * EXP_SCALE)
                acc[g] = acc[g] * jnp.concatenate([scale, scale], axis=1) + part
            m_ref[g] = new
            return carry

        lax.fori_loop(0, count, one, 0, unroll=4)

    all_heads = (0, 1, GROUP)
    loads[3].wait()

    @pl.when(z >= 2)
    def _():
        pass_down(2)

    @pl.when(z >= 3)
    def _():
        pass_down(3)

    settle(0)
    attend(z, True, (0, 2, GROUP // 2))

    @pl.when(z >= 1)
    def _():
        pass_on(1)

    attend(z, True, (1, 2, GROUP // 2))

    @pl.when(z >= 2)
    def _():
        pass_on(2)
        settle(1)
        attend(z - 1, False, (0, 2, GROUP // 2))

    @pl.when(z >= 3)
    def _():
        pass_on(3)

    @pl.when(z >= 2)
    def _():
        attend(z - 1, False, (1, 2, GROUP // 2))

    for sub in range(2):
        for step in range(1, ROW):

            @pl.when(z >= step)
            def _():
                climb_wait(1, sub, zsend, zrecv, ROW - step)

        scan_back(2, sub, zrecv, bsend, brecv, before, ahead, (0, 1, 2), lambda zz: zz < z)

    @pl.when(z >= 3)
    def _():
        settle(2)
        attend(z - 2, False, all_heads)

    for sub in range(2):
        for step in range(1, ROW):
            trade_wait(2, sub, bsend, brecv, step)
        for part in range(4):
            cut = group_cut(part, sub)
            inter[:, cut] = ecum_full[:, cut] * nn(c_rows, brecv[sub, part])

    @pl.when(z >= 1)
    def _():
        settle(z)

    skip_row = summed(nn, jnp.broadcast_to(skp[...], (8, HG)), spread)[0:1, :]

    def fold(a):
        a = a.reshape(T // 8, 8, a.shape[1])
        a = jnp.sum(a, axis=0)
        out = a[:, 0:128]
        for j in range(1, a.shape[1] // 128):
            out = out + a[:, j * 128 : (j + 1) * 128]
        return out

    def rise(sub):
        scan_row(3, sub, ysend2, yrecv2, zsend2, before, behind)
        for step in range(1, ROW):

            @pl.when(z >= step)
            def _():
                climb(4, sub, zsend2, zrecv2, ROW - step).start()

    power = jnp.zeros((8, 128), F32)
    error = jnp.zeros((8, 128), F32)
    for sub in range(2):

        @pl.when(z >= 1)
        def _():
            attend(0, False, (sub, 2, GROUP // 2))

        for part in range(4):
            cut = group_cut(part, sub)
            both = acc[2 * part + sub]
            goal = (both[:, :HD] / both[:, HD:]).astype(BF16).astype(F32)
            made = intra[:, cut] + inter[:, cut] + skip_row[:, cut] * x[:, cut].astype(F32)
            resid = made - goal
            power = power + fold(goal * goal)
            error = error + fold(resid * resid)
            up = 2.0 * resid
            ups[:, cut] = up
            upb[:, cut] = up.astype(BF16)
            eu[:, cut] = (ecum_full[:, cut] * up).astype(BF16)
            ysend2[sub, part] = nn(c_cols, eu[:, cut]).astype(BF16)
        trades(3, sub, ysend2, yrecv2)

    def spread_out(buf, place, stage, at, size):
        out = []
        for step in range(1, size):
            out.append(
                remote(
                    buf.at[pl.ds(place, 1)], buf.at[pl.ds(place, 1)], red_send.at[stage, step - 1],
                    red_recv.at[stage, place], at(step),
                )
            )
        return out

    def collect(buf, place, stage, at, size):
        for step in range(1, size):
            other = (place + step) % size
            remote(
                buf.at[pl.ds(place, 1)], buf.at[pl.ds(other, 1)], red_send.at[stage, step - 1],
                red_recv.at[stage, other], at(step),
            ).wait_recv()
        total = buf[0]
        for j in range(1, size):
            total = total + buf[j]
        return total

    def launch(value, buf, place, stage, at, size):
        buf[pl.ds(place, 1)] = value[None]
        for copy in spread_out(buf, place, stage, at, size):
            copy.start()

    launch(jnp.concatenate([power, error], axis=0), sd, d, 2, at_d, dp_size)
    for kind, weight in enumerate((weight_z, weight_y)):
        eu_like[...] = (summed(tn, weight[...], spread, 2) * x[...].astype(F32)).astype(BF16)
        for sub in range(2):
            for part in range(4):
                zysend[part, 2 * sub + kind] = nn(
                    b_cols, eu_like[:, group_cut(part, sub)]
                ).astype(BF16)

    def zy(step):
        to = (y + step) % ROW
        return remote(
            zysend.at[to], zyrecv.at[y], zy_send.at[step - 1], zy_recv.at[y], at_y(step)
        )

    def zy_wait(step):
        other = (y + step) % ROW
        remote(
            zysend.at[other], zyrecv.at[other], zy_send.at[step - 1], zy_recv.at[other], at_y(step)
        ).wait_recv()

    for step in range(1, ROW):
        zy(step).start()
    zyrecv[pl.ds(y, 1)] = zysend[pl.ds(y, 1)]
    launch(collect(sd, d, 2, at_d, dp_size), st, tt, 3, at_t, tensor_size)

    rise(0)
    rise(1)

    def pair_products(pair, running):
        ups_pair = halves(upb[:, lanes(pair, 128)])
        x_pair = x[:, lanes(pair, 128)]
        through = jnp.zeros((T, 128), F32)
        for i in range(2):
            h = 2 * pair + i
            running = running + timed[h] * nt(ups_pair[i], x_pair)
            through = through + nn(mixt[h], ups_pair[i])
        t1[:, lanes(pair, 128)] = through
        return running

    paired = lax.fori_loop(0, GROUP, pair_products, jnp.zeros((T, T), F32), unroll=2)
    launch(collect(st, tt, 3, at_t, tensor_size), sy, y, 0, at_y, ROW)

    def by_head(a):
        return summed(nt, a, spread, 2, left=False)

    heads_at = marks((CH, 128), lambda j, h: (j >> 6) == h)
    heads_next = marks((CH, 128), lambda j, h: (j >> 6) == h - HG)
    xf = x[...].astype(F32)
    through_x = xf * t1[...]
    gains = upb[...].astype(F32) * intra[...] - through_x + ups[...] * inter[...]
    stats = summed(nn, gains, heads_at, 2) + nn(through_x.astype(BF16), heads_next)
    stats = stats.T
    gained = stats[0:HG]
    from_mix = stats[HG : 2 * HG]
    skip_part = jnp.sum((ups[...] * xf).reshape(T // 8, 8, CH), axis=0)
    skip_term = jnp.sum(by_head(skip_part), axis=1, keepdims=True)
    since = marks((T, T), lambda s, t: s >= t)
    until = marks((T, T), lambda s, t: s < t)
    gained_after = summed(nn, gained, since)
    decay_local = jnp.sum(gained_after * decay, axis=1, keepdims=True)
    shift_local = jnp.sum(
        (from_mix / step_size - gained_after * rate) * gate, axis=1, keepdims=True
    )
    launch(collect(sy, y, 0, at_y, ROW), sz, z, 1, at_z, ROW)

    for step in range(1, ROW):
        zy_wait(step)
    parts = []
    for sub in range(2):
        for step in range(1, ROW):

            @pl.when(z + step < ROW)
            def _():
                climb_wait(4, sub, zsend2, zrecv2, step)

        scan_back(5, sub, zrecv2, bsend2, brecv2, before, behind, (3, 2, 1), lambda zz: zz > z)
        parts.append(functionals(sub))
    owned = marks((HG, QW), lambda h, j: h == y * 4 + (j >> 6))

    def owned_heads(kind):
        both = jnp.concatenate([parts[0][kind], parts[1][kind]], axis=1)
        return jnp.sum(summed(nt, both, owned, left=False), axis=1, keepdims=True)

    lane = iota((HG, 128), 1)
    heads = jnp.where(
        lane == 0, decay_local + owned_heads(0),
        jnp.where(lane == 1, shift_local + owned_heads(1), skip_term),
    )
    launch(heads, hd, d, 6, at_d, dp_size)

    paired_rows = paired.astype(BF16)
    paired_cols = paired.T.astype(BF16)
    grad_b = nn(paired_cols, c_rows)
    grad_c = nn(paired_rows, b_rows)
    for sub in range(2):
        for part in range(4):
            grad_c = grad_c + nt(eu[:, group_cut(part, sub)], brecv[sub, part])

    both_sums = collect(sz, z, 1, at_z, ROW)
    power_all = jnp.sum(both_sums[0:8, :], keepdims=True)
    error_all = jnp.sum(both_sums[8:16, :], keepdims=True)
    mean_square = power_all / entries + EPSILON
    factor = 1.0 / mean_square
    gls[...] = jnp.broadcast_to(error_all / mean_square / entries, (8, 128))

    overlap = [None] * 8
    later_stats = jnp.zeros((T, 128), F32)
    for sub in range(2):
        for step in range(1, ROW):
            trade_wait(5, sub, bsend2, brecv2, step)
        for part in range(4):
            cut = group_cut(part, sub)
            later = brecv2[sub, part]
            came = ts_full[:, cut] * nn(b_rows, later)
            gx[:, cut] = (
                (skip_row[:, cut] * ups[:, cut] + t1[:, cut] + came) * factor
            ).astype(BF16)
            grad_b = grad_b + nt(xs[:, cut], later)
            later_stats = later_stats + nn(
                (x[:, cut].astype(F32) * came).astype(BF16), heads_at[cut, :]
            )
            prod = later.astype(F32) * brecv[sub, part].astype(F32)
            overlap[2 * part + sub] = tiles(prod)
        if sub == 0:
            launch(collect(hd, d, 6, at_d, dp_size), hz, z, 5, at_z, ROW)
    from_later = later_stats.T[0:HG]
    meet = jnp.sum(by_head(jnp.concatenate(overlap, axis=1)), axis=1, keepdims=True)
    decay_grad = gained_after + summed(nn, from_later, until) + jnp.exp(total) * meet
    direct = (from_mix + from_later) / step_size
    shift_grad = (direct - decay_grad * rate) * gate
    gdt[...] = shift_grad * factor
    launch(collect(hz, z, 5, at_z, ROW), hy, y, 4, at_y, ROW)
    put_b = marks((2 * T, T), lambda r, t: r == 2 * t)
    put_c = marks((2 * T, T), lambda r, t: r == 2 * t + 1)
    gbc[...] = (
        nn(put_b, (grad_b * factor).astype(BF16)) + nn(put_c, (grad_c * factor).astype(BF16))
    ).astype(BF16)
    ghd[...] = collect(hy, y, 4, at_y, ROW) * factor

    for step in range(1, ROW):

        @pl.when(z + step < ROW)
        def _():
            for which in range(2):
                kv_z(step, which).wait_send()
            for sub in range(2):
                climb(1, sub, zsend, zrecv, step).wait_send()

        @pl.when(z >= step)
        def _():
            for sub in range(2):
                climb(4, sub, zsend2, zrecv2, ROW - step).wait_send()

        zy(step).wait_send()
        tot_y(step).wait_send()
        tot_z(step).wait_send()
        for sub in range(2):
            trade(0, sub, ysend, yrecv, step).wait_send()
            trade(2, sub, bsend, brecv, step).wait_send()
            trade(3, sub, ysend2, yrecv2, step).wait_send()
            trade(5, sub, bsend2, brecv2, step).wait_send()
    for back in range(ROW):

        @pl.when(z >= back)
        def _():
            for copy in y_sends(back) + forwards(back):
                copy.wait_send()

    for buf, place, stage, at, size in (
        (sy, y, 0, at_y, ROW), (sz, z, 1, at_z, ROW), (sd, d, 2, at_d, dp_size),
        (st, tt, 3, at_t, tensor_size), (hy, y, 4, at_y, ROW), (hz, z, 5, at_z, ROW),
        (hd, d, 6, at_d, dp_size),
    ):
        for copy in spread_out(buf, place, stage, at, size):
            copy.wait_send()


def write_out(gx, gbc, gdt, ghd, gls, ogx, ogbc, ogdt, oghd, ogls):
    ogx[...] = gx[...]
    ogbc[...] = gbc[...]
    ogdt[...] = gdt[...]
    turned = ghd[...].T
    for i in range(3):
        oghd[i] = turned[i : i + 1, :]
    ogls[...] = gls[0:1, 0:1]


def solution(mesh):
    dp_size, tensor_size = mesh.shape["dp"], mesh.shape["tensor"]
    entries = float(dp_size * mesh.shape["ctx"] * tensor_size * T * CH)

    def vm(shape, kind):
        return pltpu.VMEM(shape, kind)

    chunk4 = (2, ROW, N, 128)
    scratch = [
        vm((T, CH), BF16), vm((T, CH), BF16), vm((2 * T, N), BF16), vm((HG, T), F32),
        vm((16 * T, HD), BF16), vm((16 * T, HD), BF16),
        vm((GROUP, T, HD), F32), vm((GROUP, T, 2 * HD), F32),
        vm((HG, T, T), F32), vm((HG, T, T), BF16),
        vm((T, HG * 128), F32), vm((T, HG * 128), F32),
        vm((HG, T), F32), vm((HG, T), F32), vm((T, T), F32), vm((T, T), F32),
        vm((T, CH), F32), vm((T, CH), F32), vm((T, CH), BF16), vm((T, CH), F32),
        vm((T, CH), F32), vm((T, CH), F32), vm((T, CH), BF16), vm((T, CH), BF16),
        vm((T, CH), F32),
        vm((16, 8, 128), F32), vm((2, 16, 128), F32), vm((2, 16, 128), F32), vm((2, ROW, N, 128), F32),
        vm((HG, T), F32), vm((HG, T), F32), vm((T, CH), BF16),
        vm((ROW, 4, N, 128), BF16), vm((ROW, 4, N, 128), BF16),
    ]
    for _ in range(2):
        scratch += [
            vm(chunk4, BF16), vm(chunk4, BF16), vm((2, N, 128), BF16), vm(chunk4, BF16),
            vm(chunk4, BF16), vm(chunk4, BF16),
        ]
    scratch += [
        vm((ROW, 16, 128), F32), vm((ROW, 16, 128), F32), vm((dp_size, 16, 128), F32),
        vm((tensor_size, 16, 128), F32), vm((ROW, 16, 128), F32), vm((ROW, 16, 128), F32),
        vm((dp_size, 16, 128), F32),
    ]
    sem = pltpu.SemaphoreType.DMA
    scratch += [
        sem((6,)), sem((2, 16)), sem((3, 2)), sem((4, 6)),
        sem((2, 3)), sem((2, 4)), sem((6, 2, 3)), sem((6, 2, 4)), sem((7, 3)), sem((7, 4)), sem((3,)), sem((4,)),
    ]

    def body(queries, keys, values, student_x, student_bc, student_dt, a_log, dt_bias, skip):
        whole = pl.BlockSpec(memory_space=pltpu.VMEM)
        far = pl.BlockSpec(memory_space=pltpu.HBM)

        def run(*refs):
            kernel(entries, dp_size, tensor_size, *refs)

        gx, gbc, gdt, ghd, gls = pl.pallas_call(
            run,
            out_shape=(
                jax.ShapeDtypeStruct((T, CH), BF16),
                jax.ShapeDtypeStruct((2 * T, N), BF16),
                jax.ShapeDtypeStruct((HG, T), F32),
                jax.ShapeDtypeStruct((HG, 128), F32),
                jax.ShapeDtypeStruct((8, 128), F32),
            ),
            in_specs=[far] * 6 + [whole] * 3,
            out_specs=(whole,) * 5,
            scratch_shapes=scratch,
            compiler_params=pltpu.CompilerParams(
                collective_id=0, has_side_effects=True, vmem_limit_bytes=61 * 1024 * 1024
            ),
            name="align",
        )(
            queries.reshape(T, CH), keys.reshape(T, HD), values.reshape(T, HD),
            student_x.reshape(T, CH), student_bc.reshape(2 * T, N),
            student_dt.reshape(T, HG).T, a_log, dt_bias, skip,
        )
        gx, gbc, gdt, ghd, gls = pl.pallas_call(
            write_out,
            out_shape=(
                jax.ShapeDtypeStruct((T, CH), BF16),
                jax.ShapeDtypeStruct((2 * T, N), BF16),
                jax.ShapeDtypeStruct((HG, T), F32),
                jax.ShapeDtypeStruct((3, 1, HG), F32),
                jax.ShapeDtypeStruct((1, 1), F32),
            ),
            in_specs=[whole] * 5,
            out_specs=(whole,) * 5,
            compiler_params=pltpu.CompilerParams(vmem_limit_bytes=61 * 1024 * 1024),
            name="write_out",
        )(gx, gbc, gdt, ghd, gls)
        return (
            gx.reshape(1, T, 1, CH),
            gbc.reshape(1, T, 1, 2, N),
            gdt.T.reshape(1, T, 1, HG),
            ghd,
            gls.reshape(()),
        )

    return jax.shard_map(
        body,
        mesh=mesh,
        in_specs=(
            P("dp", "ctx", "tensor", None),
            P("dp", "ctx", "tensor", None),
            P("dp", "ctx", "tensor", None),
            P("dp", "ctx", "tensor", None),
            P("dp", "ctx", "tensor", None, None),
            P("dp", "ctx", "tensor", None),
            P("tensor", None),
            P("tensor", None),
            P("tensor", None),
        ),
        out_specs=(
            P("dp", "ctx", "tensor", None),
            P("dp", "ctx", "tensor", None, None),
            P("dp", "ctx", "tensor", None),
            P(None, "tensor", None),
            P(),
        ),
        check_vma=False,
    )
```

```python
import jax
import jax.numpy as jnp
from jax import lax
from jax.experimental import pallas as pl
from jax.experimental.pallas import tpu as pltpu
from jax.sharding import PartitionSpec as P

T = 256
HD = 128
GROUP = 8
N = 128
HG = 16
CH = 1024
QW = 256
ROW = 4
F32 = jnp.float32
BF16 = jnp.bfloat16
NEGATIVE = -1e30
EPSILON = 1e-06
EXP_SCALE = 1.4426950408889634 * HD**-0.5
MESH = pl.DeviceIdType.MESH


def nn(a, b):
    return lax.dot_general(a, b, (((1,), (0,)), ((), ())), preferred_element_type=F32)


def nt(a, b):
    return lax.dot_general(a, b, (((1,), (1,)), ((), ())), preferred_element_type=F32)


def tn(a, b):
    return lax.dot_general(a, b, (((0,), (0,)), ((), ())), preferred_element_type=F32)


def pieces(a, count):
    out = []
    for _ in range(count - 1):
        top = a.astype(BF16)
        out.append(top)
        a = a - top.astype(F32)
    out.append(a.astype(BF16))
    return out


def summed(form, values, marks, count=3, left=True):
    total = None
    for part in pieces(values, count):
        term = form(part, marks) if left else form(marks, part)
        total = term if total is None else total + term
    return total


def iota(shape, dim):
    return lax.broadcasted_iota(jnp.int32, shape, dim)


def marks(shape, test):
    return jnp.where(test(iota(shape, 0), iota(shape, 1)), 1.0, 0.0).astype(BF16)


def column(ref):
    wide = jnp.broadcast_to(ref[...], (HG, HG))
    same = iota((HG, HG), 0) == iota((HG, HG), 1)
    return jnp.sum(jnp.where(same, wide, 0.0), axis=1, keepdims=True)


def kernel(
    entries, dp_size, tensor_size,
    q_in, k, v, x_in, bc_in, dt_in, alog, dtb, skp,
    gx, gbc, gdt, ghd, gls,
    q, x, bc, dt, kbuf, vbuf, m_ref, acc, timed, mixt, cumb, stepb, cumt, stept, wmat, wtmat,
    intra, inter, upb, ups, ts_full, ecum_full, xs, eu, t1,
    tot, tq, tqo, gqo, before, weight_z, weight_y, eu_like, zysend, zyrecv,
    ysend, yrecv, zsend, zrecv, bsend, brecv,
    ysend2, yrecv2, zsend2, zrecv2, bsend2, brecv2,
    sy, sz, sd, st, hy, hz, hd,
    own_sem, kv_recv, kvz_send, kvy_send,
    tot_send, tot_recv, scan_send, scan_recv, red_send, red_recv, zy_send, zy_recv,
):
    c = lax.axis_index("ctx")
    d = lax.axis_index("dp")
    tt = lax.axis_index("tensor")
    z = c // ROW
    y = c % ROW

    def at_y(step):
        return {"ctx": z * ROW + (y + step) % ROW}

    def at_z(step):
        return {"ctx": ((z + step) % ROW) * ROW + y}

    def at_d(step):
        return {"dp": (d + step) % dp_size}

    def at_t(step):
        return {"tensor": (tt + step) % tensor_size}

    peers = [at_y(s) for s in range(1, ROW)] + [at_z(s) for s in range(1, ROW)]
    peers += [at_d(s) for s in range(1, dp_size)] + [at_t(s) for s in range(1, tensor_size)]

    zrecv[...] = jnp.zeros_like(zrecv)
    zrecv2[...] = jnp.zeros_like(zrecv2)

    barrier = pltpu.get_barrier_semaphore()
    for peer in peers:
        pl.semaphore_signal(barrier, inc=1, device_id=peer, device_id_type=MESH)

    def rows(slot):
        return pl.ds(pl.multiple_of(slot * T, T), T)

    own_k = pltpu.make_async_copy(k, kbuf.at[rows(c)], own_sem.at[0])
    own_v = pltpu.make_async_copy(v, vbuf.at[rows(c)], own_sem.at[1])
    loads = [
        pltpu.make_async_copy(src, dst, own_sem.at[2 + i])
        for i, (src, dst) in enumerate(((dt_in, dt), (bc_in, bc), (x_in, x), (q_in, q)))
    ]
    for copy in [own_k, own_v] + loads:
        copy.start()
    pl.semaphore_wait(barrier, len(peers))

    def remote(src, dst, send, recv, peer):
        return pltpu.make_async_remote_copy(
            src_ref=src, dst_ref=dst, send_sem=send, recv_sem=recv,
            device_id=peer, device_id_type=MESH,
        )

    bufs = (kbuf, vbuf)

    def kv_z(step, which):
        return remote(
            (k, v)[which], bufs[which].at[rows(c)], kvz_send.at[step - 1, which],
            kv_recv.at[which, c], at_z(step),
        )

    def kv_y(back, lane, which, slot, step):
        return remote(
            bufs[which].at[rows(slot)], bufs[which].at[rows(slot)], kvy_send.at[back, lane],
            kv_recv.at[which, slot], at_y(step),
        )

    def kv_wait(which, slot):
        remote(
            bufs[which].at[rows(slot)], bufs[which].at[rows(slot)], own_sem.at[which],
            kv_recv.at[which, slot], at_y(1),
        ).wait_recv()

    def y_sends(back):
        slot = (z - back) * ROW + y
        return [
            kv_y(back, 0, 0, slot, 1), kv_y(back, 1, 1, slot, 3),
            kv_y(back, 2, 1, slot, 1), kv_y(back, 3, 0, slot, 3),
        ]

    def slot_of(back, step):
        return (z - back) * ROW + (y + step) % ROW

    def forwards(back):
        return [kv_y(back, 4, 0, slot_of(back, 3), 1), kv_y(back, 5, 1, slot_of(back, 1), 3)]

    for step in (1, 2, 3):

        @pl.when(z + step < ROW)
        def _():
            for which in range(2):
                kv_z(step, which).start()

    own_k.wait()
    own_v.wait()
    for copy in y_sends(0):
        copy.start()

    def pass_down(back):
        for which in range(2):
            kv_wait(which, slot_of(back, 0))
        for copy in y_sends(back):
            copy.start()

    def pass_on(back):
        kv_wait(0, slot_of(back, 3))
        kv_wait(1, slot_of(back, 1))
        for copy in forwards(back):
            copy.start()

    def settle(back):
        kv_wait(1, slot_of(back, 3))
        kv_wait(0, slot_of(back, 1))
        for which in range(2):
            kv_wait(which, slot_of(back, 2))

    def group_cut(part, sub):
        g = 2 * part + sub
        return slice(g * 128, (g + 1) * 128)

    for copy in loads[:3]:
        copy.wait()
    bias = column(dtb)
    rate = jnp.exp(column(alog))
    shifted = dt[...] + bias
    step_size = jnp.maximum(shifted, 0.0) + jnp.log1p(jnp.exp(-jnp.abs(shifted)))
    decay = -step_size * rate
    upto = marks((T, T), lambda s, t: s <= t)
    same = marks((T, T), lambda s, t: s == t)
    cum_t = summed(nn, decay, upto)
    cum_c = summed(nt, cum_t, same, left=False)
    total = cum_t[:, T - 1 : T]
    cumt[...] = cum_t
    stept[...] = step_size
    spread = marks((HG, CH), lambda h, j: (j >> 6) == h)
    tail_step = jnp.exp(total - cum_t) * step_size
    ts_full[...] = summed(tn, tail_step, spread, 2)
    xs[...] = (ts_full[...] * x[...].astype(F32)).astype(BF16)
    pick_b = marks((T, 2 * T), lambda t, r: r == 2 * t)
    pick_c = marks((T, 2 * T), lambda t, r: r == 2 * t + 1)
    b_f = nn(pick_b, bc[...])
    c_f = nn(pick_c, bc[...])
    b_rows = b_f.astype(BF16)
    c_rows = c_f.astype(BF16)
    b_cols = b_f.T.astype(BF16)
    c_cols = c_f.T.astype(BF16)

    gate = 1.0 / (1.0 + jnp.exp(-shifted))
    later_than = marks((T, T), lambda s, t: s > t)
    gate_after = summed(nn, gate, later_than)
    gate_sum = jnp.broadcast_to(jnp.sum(gate, axis=1, keepdims=True) * rate, (HG, 128))
    gate_row = jnp.sum(
        jnp.where(iota((HG, 128), 1) == iota((HG, 128), 0) + HG, gate_sum, 0.0),
        axis=0, keepdims=True,
    )
    total_row = jnp.sum(
        jnp.where(
            iota((HG, 128), 1) == iota((HG, 128), 0), jnp.broadcast_to(total, (HG, 128)), 0.0
        ),
        axis=0, keepdims=True,
    )
    tot[pl.ds(c, 1)] = jnp.broadcast_to((total_row + gate_row)[None], (1, 8, 128))
    weight_z[...] = tail_step * (total - cum_t)
    weight_y[...] = tail_step * (gate / step_size - rate * gate_after)
    for sub in range(2):
        for part in range(4):
            ysend[sub, part] = nn(b_cols, xs[:, group_cut(part, sub)]).astype(BF16)

    def tot_y(step):
        return remote(
            tot.at[pl.ds(c, 1)], tot.at[pl.ds(c, 1)], tot_send.at[0, step - 1],
            tot_recv.at[0, y], at_y(step),
        )

    def tot_y_wait(step):
        other = (y + step) % ROW
        remote(
            tot.at[pl.ds(c, 1)], tot.at[pl.ds(z * ROW + other, 1)], tot_send.at[0, step - 1],
            tot_recv.at[0, other], at_y(step),
        ).wait_recv()

    def tot_z(step):
        return remote(
            tot.at[pl.ds(z * ROW, ROW)], tot.at[pl.ds(z * ROW, ROW)], tot_send.at[1, step - 1],
            tot_recv.at[1, z], at_z(step),
        )

    def tot_z_wait(step):
        other = (z + step) % ROW
        remote(
            tot.at[pl.ds(z * ROW, ROW)], tot.at[pl.ds(other * ROW, ROW)], tot_send.at[1, step - 1],
            tot_recv.at[1, other], at_z(step),
        ).wait_recv()

    def trade(phase, sub, src, dst, step):
        to = (y + step) % ROW
        return remote(
            src.at[sub, to], dst.at[sub, y], scan_send.at[phase, sub, step - 1],
            scan_recv.at[phase, sub, y], at_y(step),
        )

    def trade_wait(phase, sub, src, dst, step):
        other = (y + step) % ROW
        remote(
            src.at[sub, other], dst.at[sub, other], scan_send.at[phase, sub, step - 1],
            scan_recv.at[phase, sub, other], at_y(step),
        ).wait_recv()

    def climb(phase, sub, src, dst, step):
        return remote(
            src.at[sub], dst.at[sub, z], scan_send.at[phase, sub, step - 1],
            scan_recv.at[phase, sub, z], at_z(step),
        )

    def climb_wait(phase, sub, src, dst, step):
        other = (z + step) % ROW
        remote(
            src.at[sub], dst.at[sub, other], scan_send.at[phase, sub, step - 1],
            scan_recv.at[phase, sub, other], at_z(step),
        ).wait_recv()

    def trades(phase, sub, src, dst):
        for step in (2, 1, 3):
            trade(phase, sub, src, dst, step).start()
        dst[sub, pl.ds(y, 1)] = src[sub, pl.ds(y, 1)]

    for step in range(1, ROW):
        tot_y(step).start()
    for sub in range(2):
        trades(0, sub, ysend, yrecv)

    wmat[...] = nt(c_rows, b_rows)
    wtmat[...] = nt(b_rows, c_rows)
    step_c = summed(nt, step_size, same, left=False)
    for h in range(HG):
        cumb[:, h * 128 : (h + 1) * 128] = jnp.broadcast_to(cum_c[:, h : h + 1], (T, 128))
        stepb[:, h * 128 : (h + 1) * 128] = jnp.broadcast_to(step_c[:, h : h + 1], (T, 128))
    ecum_full[...] = summed(tn, jnp.exp(cum_t), spread, 2)

    low_half = iota((T, 128), 1) < 64
    zero_pair = jnp.zeros((T, 128), BF16)

    def halves(pair):
        return jnp.where(low_half, pair, zero_pair), jnp.where(low_half, zero_pair, pair)

    def lanes(index, width):
        return pl.ds(pl.multiple_of(index * width, width), width)

    def mix_pair(pair, carry):
        lower = iota((T, T), 0) >= iota((T, T), 1)
        upper = iota((T, T), 0) <= iota((T, T), 1)
        parts = halves(x[:, lanes(pair, 128)])
        result = jnp.zeros((T, 128), F32)
        for i in range(2):
            h = 2 * pair + i
            at_t = cumb[:, lanes(h, 128)]
            at_t = jnp.concatenate([at_t, at_t], axis=1)
            size_c = stepb[:, lanes(h, 128)]
            size_c = jnp.concatenate([size_c, size_c], axis=1)
            at_s = cumt[pl.ds(h, 1), :]
            size_r = stept[pl.ds(h, 1), :]
            held = jnp.exp(jnp.where(lower, at_t - at_s, NEGATIVE)) * size_r
            timed[h] = held
            mixed = (held * wmat[...]).astype(BF16)
            result = result + nn(mixed, parts[i])
            turned = jnp.exp(jnp.where(upper, at_s - at_t, NEGATIVE)) * size_c
            mixt[h] = (turned * wtmat[...]).astype(BF16)
        intra[:, lanes(pair, 128)] = result
        return carry


    @pl.when(z >= 1)
    def _():
        pass_down(1)

    pass_on(0)
    lax.fori_loop(0, GROUP // 2, mix_pair, 0)
    for step in range(1, ROW):
        tot_y_wait(step)
    for step in range(1, ROW):
        tot_z(step).start()
    lax.fori_loop(GROUP // 2, GROUP, mix_pair, 0)

    mine = marks((128, QW), lambda h, j: h == y * 4 + (j >> 6))
    mine_next = marks((128, QW), lambda h, j: h == HG + y * 4 + (j >> 6))
    row_tot = jnp.sum(
        jnp.where(iota((ROW, 8, 128), 1) == 0, tot[pl.ds(z * ROW, ROW)], 0.0), axis=1
    )
    row_tot = jnp.concatenate([row_tot, row_tot], axis=0)
    own_tot = summed(nn, row_tot, mine)
    own_gate = summed(nn, row_tot, mine_next)
    for sub in range(2):
        tqo[sub] = own_tot[:, sub * 128 : (sub + 1) * 128]
        gqo[sub] = own_gate[:, sub * 128 : (sub + 1) * 128]

    def own_total(sub, kk):
        return tqo[sub, kk : kk + 1, :]

    def total_of(sub, zz, kk):
        return tq[sub, zz * ROW + kk : zz * ROW + kk + 1, :]

    def row_total(sub, zz):
        return sum(total_of(sub, zz, kk) for kk in range(1, ROW)) + total_of(sub, zz, 0)

    def scan_row(phase, sub, src, got, up, pre, order):
        for step in range(1, ROW):
            trade_wait(phase, sub, src, got, step)
        run = jnp.zeros((N, 128), F32)
        for kk in order:
            pre[sub, kk] = run
            run = jnp.exp(own_total(sub, kk)) * run + got[sub, kk].astype(F32)
        up[sub] = run.astype(BF16)

    def scan_back(phase, sub, got, back, final, pre, order, rows_in, arrived):
        held = jnp.zeros((N, 128), F32)
        for zz in rows_in:
            held = jnp.where(
                arrived(zz), jnp.exp(row_total(sub, zz)) * held + got[sub, zz].astype(F32), held
            )
        passed = jnp.zeros((1, 128), F32)
        for kk in order:
            back[sub, kk] = (jnp.exp(passed) * held + pre[sub, kk]).astype(BF16)
            passed = passed + own_total(sub, kk)
        trades(phase, sub, back, final)

    def tiles(a):
        return jnp.sum(a.reshape(N // 8, 8, 128), axis=0)

    def functionals(sub):
        for_decay = jnp.zeros((8, 128), F32)
        for_shift = jnp.zeros((8, 128), F32)
        for kk in range(ROW):
            later = bsend2[sub, kk].astype(F32)
            sofar = own_total(sub, kk)
            met = jnp.exp(sofar) * tiles(later * bsend[sub, kk].astype(F32))
            gates = gqo[sub, kk : kk + 1, :]
            for_decay = for_decay + tiles(later * zyrecv[kk, 2 * sub].astype(F32)) + sofar * met
            for_shift = for_shift + tiles(later * zyrecv[kk, 2 * sub + 1].astype(F32)) - gates * met
        return for_decay, for_shift

    ahead = (0, 1, 2, 3)
    behind = (3, 2, 1, 0)
    for sub in range(2):
        scan_row(0, sub, ysend, yrecv, zsend, before, ahead)
        for step in range(1, ROW):

            @pl.when(z + step < ROW)
            def _():
                climb(1, sub, zsend, zrecv, step).start()

    ones = jnp.ones((ROW * T, HD), BF16)

    def attend(row, first, heads):
        base = pl.multiple_of(row * (ROW * T), ROW * T)
        start, stride, count = heads

        def one(i, carry):
            g = start + stride * i
            keys = kbuf[pl.ds(base, ROW * T), :]
            both = jnp.concatenate([vbuf[pl.ds(base, ROW * T), :], ones], axis=1)
            scores = nt(q[:, lanes(g, HD)], keys)
            if first:
                seen = iota((T, ROW * T), 1) <= iota((T, ROW * T), 0) + y * T
                scores = jnp.where(seen, scores, NEGATIVE)
            top = jnp.max(scores, axis=1, keepdims=True)
            if first:
                new = jnp.broadcast_to(top, (T, HD))
            else:
                old = m_ref[g]
                new = jnp.maximum(old, top)
            weights = jnp.exp2((scores - jnp.concatenate([new] * 8, axis=1)) * EXP_SCALE)
            part = nn(weights.astype(BF16), both)
            if first:
                acc[g] = part
            else:
                scale = jnp.exp2((old - new) * EXP_SCALE)
                acc[g] = acc[g] * jnp.concatenate([scale, scale], axis=1) + part
            m_ref[g] = new
            return carry

        lax.fori_loop(0, count, one, 0, unroll=4)

    all_heads = (0, 1, GROUP)
    loads[3].wait()

    @pl.when(z >= 2)
    def _():
        pass_down(2)

    @pl.when(z >= 3)
    def _():
        pass_down(3)

    settle(0)
    attend(z, True, (0, 2, GROUP // 2))

    @pl.when(z >= 1)
    def _():
        pass_on(1)

    attend(z, True, (1, 2, GROUP // 2))

    @pl.when(z >= 2)
    def _():
        pass_on(2)
        settle(1)
        attend(z - 1, False, (0, 2, GROUP // 2))

    @pl.when(z >= 3)
    def _():
        pass_on(3)

    @pl.when(z >= 2)
    def _():
        attend(z - 1, False, (1, 2, GROUP // 2))

    for step in range(1, ROW):
        tot_z_wait(step)
    totals = jnp.sum(jnp.where(iota((16, 8, 128), 1) == 0, tot[...], 0.0), axis=1)
    all_tot = summed(nn, totals, mine)
    for sub in range(2):
        tq[sub] = all_tot[:, sub * 128 : (sub + 1) * 128]

    for sub in range(2):
        for step in range(1, ROW):

            @pl.when(z >= step)
            def _():
                climb_wait(1, sub, zsend, zrecv, ROW - step)

        scan_back(2, sub, zrecv, bsend, brecv, before, ahead, (0, 1, 2), lambda zz: zz < z)

    @pl.when(z >= 3)
    def _():
        settle(2)
        attend(z - 2, False, all_heads)

    for sub in range(2):
        for step in range(1, ROW):
            trade_wait(2, sub, bsend, brecv, step)
        for part in range(4):
            cut = group_cut(part, sub)
            inter[:, cut] = ecum_full[:, cut] * nn(c_rows, brecv[sub, part])

    @pl.when(z >= 1)
    def _():
        settle(z)

    skip_row = summed(nn, jnp.broadcast_to(skp[...], (8, HG)), spread)[0:1, :]

    def fold(a):
        a = a.reshape(T // 8, 8, a.shape[1])
        a = jnp.sum(a, axis=0)
        out = a[:, 0:128]
        for j in range(1, a.shape[1] // 128):
            out = out + a[:, j * 128 : (j + 1) * 128]
        return out

    def rise(sub):
        scan_row(3, sub, ysend2, yrecv2, zsend2, before, behind)
        for step in range(1, ROW):

            @pl.when(z >= step)
            def _():
                climb(4, sub, zsend2, zrecv2, ROW - step).start()

    power = jnp.zeros((8, 128), F32)
    error = jnp.zeros((8, 128), F32)
    for sub in range(2):

        @pl.when(z >= 1)
        def _():
            attend(0, False, (sub, 2, GROUP // 2))

        for part in range(4):
            cut = group_cut(part, sub)
            both = acc[2 * part + sub]
            goal = (both[:, :HD] / both[:, HD:]).astype(BF16).astype(F32)
            made = intra[:, cut] + inter[:, cut] + skip_row[:, cut] * x[:, cut].astype(F32)
            resid = made - goal
            power = power + fold(goal * goal)
            error = error + fold(resid * resid)
            up = 2.0 * resid
            ups[:, cut] = up
            upb[:, cut] = up.astype(BF16)
            eu[:, cut] = (ecum_full[:, cut] * up).astype(BF16)
            ysend2[sub, part] = nn(c_cols, eu[:, cut]).astype(BF16)
        trades(3, sub, ysend2, yrecv2)

    def spread_out(buf, place, stage, at, size):
        out = []
        for step in range(1, size):
            out.append(
                remote(
                    buf.at[pl.ds(place, 1)], buf.at[pl.ds(place, 1)], red_send.at[stage, step - 1],
                    red_recv.at[stage, place], at(step),
                )
            )
        return out

    def collect(buf, place, stage, at, size):
        for step in range(1, size):
            other = (place + step) % size
            remote(
                buf.at[pl.ds(place, 1)], buf.at[pl.ds(other, 1)], red_send.at[stage, step - 1],
                red_recv.at[stage, other], at(step),
            ).wait_recv()
        total = buf[0]
        for j in range(1, size):
            total = total + buf[j]
        return total

    def launch(value, buf, place, stage, at, size):
        buf[pl.ds(place, 1)] = value[None]
        for copy in spread_out(buf, place, stage, at, size):
            copy.start()

    launch(jnp.concatenate([power, error], axis=0), sd, d, 2, at_d, dp_size)
    for kind, weight in enumerate((weight_z, weight_y)):
        eu_like[...] = (summed(tn, weight[...], spread, 2) * x[...].astype(F32)).astype(BF16)
        for sub in range(2):
            for part in range(4):
                zysend[part, 2 * sub + kind] = nn(
                    b_cols, eu_like[:, group_cut(part, sub)]
                ).astype(BF16)

    def zy(step):
        to = (y + step) % ROW
        return remote(
            zysend.at[to], zyrecv.at[y], zy_send.at[step - 1], zy_recv.at[y], at_y(step)
        )

    def zy_wait(step):
        other = (y + step) % ROW
        remote(
            zysend.at[other], zyrecv.at[other], zy_send.at[step - 1], zy_recv.at[other], at_y(step)
        ).wait_recv()

    for step in range(1, ROW):
        zy(step).start()
    zyrecv[pl.ds(y, 1)] = zysend[pl.ds(y, 1)]

    rise(0)
    rise(1)
    launch(collect(sd, d, 2, at_d, dp_size), st, tt, 3, at_t, tensor_size)

    def pair_products(pair, running):
        ups_pair = halves(upb[:, lanes(pair, 128)])
        x_pair = x[:, lanes(pair, 128)]
        through = jnp.zeros((T, 128), F32)
        for i in range(2):
            h = 2 * pair + i
            running = running + timed[h] * nt(ups_pair[i], x_pair)
            through = through + nn(mixt[h], ups_pair[i])
        t1[:, lanes(pair, 128)] = through
        return running

    paired = lax.fori_loop(0, GROUP, pair_products, jnp.zeros((T, T), F32), unroll=2)

    def by_head(a):
        return summed(nt, a, spread, 2, left=False)

    heads_at = marks((CH, 128), lambda j, h: (j >> 6) == h)
    heads_next = marks((CH, 128), lambda j, h: (j >> 6) == h - HG)
    xf = x[...].astype(F32)
    through_x = xf * t1[...]
    gains = upb[...].astype(F32) * intra[...] - through_x + ups[...] * inter[...]
    stats = summed(nn, gains, heads_at, 2) + nn(through_x.astype(BF16), heads_next)
    stats = stats.T
    gained = stats[0:HG]
    from_mix = stats[HG : 2 * HG]
    skip_part = jnp.sum((ups[...] * xf).reshape(T // 8, 8, CH), axis=0)
    skip_term = jnp.sum(by_head(skip_part), axis=1, keepdims=True)
    since = marks((T, T), lambda s, t: s >= t)
    until = marks((T, T), lambda s, t: s < t)
    gained_after = summed(nn, gained, since)
    decay_local = jnp.sum(gained_after * decay, axis=1, keepdims=True)
    shift_local = jnp.sum(
        (from_mix / step_size - gained_after * rate) * gate, axis=1, keepdims=True
    )
    paired_rows = paired.astype(BF16)
    paired_cols = paired.T.astype(BF16)
    grad_b = nn(paired_cols, c_rows)
    grad_c = nn(paired_rows, b_rows)
    for sub in range(2):
        for part in range(4):
            grad_c = grad_c + nt(eu[:, group_cut(part, sub)], brecv[sub, part])

    launch(collect(st, tt, 3, at_t, tensor_size), sz, z, 1, at_z, ROW)

    for step in range(1, ROW):
        zy_wait(step)
    for sub in range(2):
        for step in range(1, ROW):

            @pl.when(z + step < ROW)
            def _():
                climb_wait(4, sub, zsend2, zrecv2, step)

        scan_back(5, sub, zrecv2, bsend2, brecv2, before, behind, (3, 2, 1), lambda zz: zz > z)
    parts = [functionals(0), functionals(1)]
    owned = marks((HG, QW), lambda h, j: h == y * 4 + (j >> 6))

    def owned_heads(kind):
        both = jnp.concatenate([parts[0][kind], parts[1][kind]], axis=1)
        return jnp.sum(summed(nt, both, owned, left=False), axis=1, keepdims=True)

    lane = iota((HG, 128), 1)
    heads = jnp.where(
        lane == 0, decay_local + owned_heads(0),
        jnp.where(lane == 1, shift_local + owned_heads(1), skip_term),
    )
    launch(heads, hd, d, 6, at_d, dp_size)

    launch(collect(sz, z, 1, at_z, ROW), sy, y, 0, at_y, ROW)
    launch(collect(hd, d, 6, at_d, dp_size), hz, z, 5, at_z, ROW)
    overlap = [None] * 8
    later_stats = jnp.zeros((T, 128), F32)
    for sub in range(2):
        for step in range(1, ROW):
            trade_wait(5, sub, bsend2, brecv2, step)
        for part in range(4):
            cut = group_cut(part, sub)
            later = brecv2[sub, part]
            came = ts_full[:, cut] * nn(b_rows, later)
            inter[:, cut] = skip_row[:, cut] * ups[:, cut] + t1[:, cut] + came
            grad_b = grad_b + nt(xs[:, cut], later)
            later_stats = later_stats + nn(
                (x[:, cut].astype(F32) * came).astype(BF16), heads_at[cut, :]
            )
            prod = later.astype(F32) * brecv[sub, part].astype(F32)
            overlap[2 * part + sub] = tiles(prod)
        if sub == 0:
            launch(collect(hz, z, 5, at_z, ROW), hy, y, 4, at_y, ROW)
    from_later = later_stats.T[0:HG]
    meet = jnp.sum(by_head(jnp.concatenate(overlap, axis=1)), axis=1, keepdims=True)
    decay_grad = gained_after + summed(nn, from_later, until) + jnp.exp(total) * meet
    direct = (from_mix + from_later) / step_size
    shift_grad = (direct - decay_grad * rate) * gate
    both_sums = collect(sy, y, 0, at_y, ROW)
    power_all = jnp.sum(both_sums[0:8, :], keepdims=True)
    error_all = jnp.sum(both_sums[8:16, :], keepdims=True)
    mean_square = power_all / entries + EPSILON
    factor = 1.0 / mean_square
    gls[...] = jnp.broadcast_to(error_all / mean_square / entries, (8, 128))

    gx[...] = (inter[...] * factor).astype(BF16)
    gdt[...] = shift_grad * factor
    put_b = marks((2 * T, T), lambda r, t: r == 2 * t)
    put_c = marks((2 * T, T), lambda r, t: r == 2 * t + 1)
    gbc[...] = (
        nn(put_b, (grad_b * factor).astype(BF16)) + nn(put_c, (grad_c * factor).astype(BF16))
    ).astype(BF16)
    ghd[...] = collect(hy, y, 4, at_y, ROW) * factor

    for step in range(1, ROW):

        @pl.when(z + step < ROW)
        def _():
            for which in range(2):
                kv_z(step, which).wait_send()
            for sub in range(2):
                climb(1, sub, zsend, zrecv, step).wait_send()

        @pl.when(z >= step)
        def _():
            for sub in range(2):
                climb(4, sub, zsend2, zrecv2, ROW - step).wait_send()

        zy(step).wait_send()
        tot_y(step).wait_send()
        tot_z(step).wait_send()
        for sub in range(2):
            trade(0, sub, ysend, yrecv, step).wait_send()
            trade(2, sub, bsend, brecv, step).wait_send()
            trade(3, sub, ysend2, yrecv2, step).wait_send()
            trade(5, sub, bsend2, brecv2, step).wait_send()
    for back in range(ROW):

        @pl.when(z >= back)
        def _():
            for copy in y_sends(back) + forwards(back):
                copy.wait_send()

    for buf, place, stage, at, size in (
        (sy, y, 0, at_y, ROW), (sz, z, 1, at_z, ROW), (sd, d, 2, at_d, dp_size),
        (st, tt, 3, at_t, tensor_size), (hy, y, 4, at_y, ROW), (hz, z, 5, at_z, ROW),
        (hd, d, 6, at_d, dp_size),
    ):
        for copy in spread_out(buf, place, stage, at, size):
            copy.wait_send()


def write_out(gx, gbc, gdt, ghd, gls, ogx, ogbc, ogdt, oghd, ogls):
    ogx[...] = gx[...]
    ogbc[...] = gbc[...]
    ogdt[...] = gdt[...]
    turned = ghd[...].T
    for i in range(3):
        oghd[i] = turned[i : i + 1, :]
    ogls[...] = gls[0:1, 0:1]


def solution(mesh):
    dp_size, tensor_size = mesh.shape["dp"], mesh.shape["tensor"]
    entries = float(dp_size * mesh.shape["ctx"] * tensor_size * T * CH)

    def vm(shape, kind):
        return pltpu.VMEM(shape, kind)

    chunk4 = (2, ROW, N, 128)
    scratch = [
        vm((T, CH), BF16), vm((T, CH), BF16), vm((2 * T, N), BF16), vm((HG, T), F32),
        vm((16 * T, HD), BF16), vm((16 * T, HD), BF16),
        vm((GROUP, T, HD), F32), vm((GROUP, T, 2 * HD), F32),
        vm((HG, T, T), F32), vm((HG, T, T), BF16),
        vm((T, HG * 128), F32), vm((T, HG * 128), F32),
        vm((HG, T), F32), vm((HG, T), F32), vm((T, T), F32), vm((T, T), F32),
        vm((T, CH), F32), vm((T, CH), F32), vm((T, CH), BF16), vm((T, CH), F32),
        vm((T, CH), F32), vm((T, CH), F32), vm((T, CH), BF16), vm((T, CH), BF16),
        vm((T, CH), F32),
        vm((16, 8, 128), F32), vm((2, 16, 128), F32), vm((2, 8, 128), F32), vm((2, 8, 128), F32),
        vm((2, ROW, N, 128), F32),
        vm((HG, T), F32), vm((HG, T), F32), vm((T, CH), BF16),
        vm((ROW, 4, N, 128), BF16), vm((ROW, 4, N, 128), BF16),
    ]
    for _ in range(2):
        scratch += [
            vm(chunk4, BF16), vm(chunk4, BF16), vm((2, N, 128), BF16), vm(chunk4, BF16),
            vm(chunk4, BF16), vm(chunk4, BF16),
        ]
    scratch += [
        vm((ROW, 16, 128), F32), vm((ROW, 16, 128), F32), vm((dp_size, 16, 128), F32),
        vm((tensor_size, 16, 128), F32), vm((ROW, 16, 128), F32), vm((ROW, 16, 128), F32),
        vm((dp_size, 16, 128), F32),
    ]
    sem = pltpu.SemaphoreType.DMA
    scratch += [
        sem((6,)), sem((2, 16)), sem((3, 2)), sem((4, 6)),
        sem((2, 3)), sem((2, 4)), sem((6, 2, 3)), sem((6, 2, 4)), sem((7, 3)), sem((7, 4)), sem((3,)), sem((4,)),
    ]

    def body(queries, keys, values, student_x, student_bc, student_dt, a_log, dt_bias, skip):
        whole = pl.BlockSpec(memory_space=pltpu.VMEM)
        far = pl.BlockSpec(memory_space=pltpu.HBM)

        def run(*refs):
            kernel(entries, dp_size, tensor_size, *refs)

        gx, gbc, gdt, ghd, gls = pl.pallas_call(
            run,
            out_shape=(
                jax.ShapeDtypeStruct((T, CH), BF16),
                jax.ShapeDtypeStruct((2 * T, N), BF16),
                jax.ShapeDtypeStruct((HG, T), F32),
                jax.ShapeDtypeStruct((HG, 128), F32),
                jax.ShapeDtypeStruct((8, 128), F32),
            ),
            in_specs=[far] * 6 + [whole] * 3,
            out_specs=(whole,) * 5,
            scratch_shapes=scratch,
            compiler_params=pltpu.CompilerParams(
                collective_id=0, has_side_effects=True, vmem_limit_bytes=61 * 1024 * 1024
            ),
            name="align",
        )(
            queries.reshape(T, CH), keys.reshape(T, HD), values.reshape(T, HD),
            student_x.reshape(T, CH), student_bc.reshape(2 * T, N),
            student_dt.reshape(T, HG).T, a_log, dt_bias, skip,
        )
        gx, gbc, gdt, ghd, gls = pl.pallas_call(
            write_out,
            out_shape=(
                jax.ShapeDtypeStruct((T, CH), BF16),
                jax.ShapeDtypeStruct((2 * T, N), BF16),
                jax.ShapeDtypeStruct((HG, T), F32),
                jax.ShapeDtypeStruct((3, 1, HG), F32),
                jax.ShapeDtypeStruct((1, 1), F32),
            ),
            in_specs=[whole] * 5,
            out_specs=(whole,) * 5,
            compiler_params=pltpu.CompilerParams(vmem_limit_bytes=61 * 1024 * 1024),
            name="write_out",
        )(gx, gbc, gdt, ghd, gls)
        return (
            gx.reshape(1, T, 1, CH),
            gbc.reshape(1, T, 1, 2, N),
            gdt.T.reshape(1, T, 1, HG),
            ghd,
            gls.reshape(()),
        )

    return jax.shard_map(
        body,
        mesh=mesh,
        in_specs=(
            P("dp", "ctx", "tensor", None),
            P("dp", "ctx", "tensor", None),
            P("dp", "ctx", "tensor", None),
            P("dp", "ctx", "tensor", None),
            P("dp", "ctx", "tensor", None, None),
            P("dp", "ctx", "tensor", None),
            P("tensor", None),
            P("tensor", None),
            P("tensor", None),
        ),
        out_specs=(
            P("dp", "ctx", "tensor", None),
            P("dp", "ctx", "tensor", None, None),
            P("dp", "ctx", "tensor", None),
            P(None, "tensor", None),
            P(),
        ),
        check_vma=False,
    )
```

```python
import jax
import jax.numpy as jnp
from jax import lax
from jax.experimental import pallas as pl
from jax.experimental.pallas import tpu as pltpu
from jax.sharding import PartitionSpec as P

T = 256
HD = 128
GROUP = 8
N = 128
HG = 16
CH = 1024
QW = 256
ROW = 4
F32 = jnp.float32
BF16 = jnp.bfloat16
NEGATIVE = -1e30
EPSILON = 1e-06
EXP_SCALE = 1.4426950408889634 * HD**-0.5
MESH = pl.DeviceIdType.MESH


def nn(a, b):
    return lax.dot_general(a, b, (((1,), (0,)), ((), ())), preferred_element_type=F32)


def nt(a, b):
    return lax.dot_general(a, b, (((1,), (1,)), ((), ())), preferred_element_type=F32)


def tn(a, b):
    return lax.dot_general(a, b, (((0,), (0,)), ((), ())), preferred_element_type=F32)


def pieces(a, count):
    out = []
    for _ in range(count - 1):
        top = a.astype(BF16)
        out.append(top)
        a = a - top.astype(F32)
    out.append(a.astype(BF16))
    return out


def summed(form, values, marks, count=3, left=True):
    total = None
    for part in pieces(values, count):
        term = form(part, marks) if left else form(marks, part)
        total = term if total is None else total + term
    return total


def iota(shape, dim):
    return lax.broadcasted_iota(jnp.int32, shape, dim)


def marks(shape, test):
    return jnp.where(test(iota(shape, 0), iota(shape, 1)), 1.0, 0.0).astype(BF16)


def column(ref):
    wide = jnp.broadcast_to(ref[...], (HG, HG))
    same = iota((HG, HG), 0) == iota((HG, HG), 1)
    return jnp.sum(jnp.where(same, wide, 0.0), axis=1, keepdims=True)


def kernel(
    entries, dp_size, tensor_size,
    q_in, k, v, x_in, bc_in, dt_in, alog, dtb, skp,
    gx, gbc, gdt, ghd, gls,
    q, x, bc, dt, kbuf, vbuf, m_ref, acc, timed, mixt, cumb, stepb, cumt, stept, wmat, wtmat,
    intra, inter, upb, ups, ts_full, ecum_full, xs, eu, t1,
    tot, tq, tqo, gqo, before, weight_z, weight_y, eu_like, zysend, zyrecv,
    ysend, yrecv, zsend, zrecv, bsend, brecv,
    ysend2, yrecv2, zsend2, zrecv2, bsend2, brecv2,
    sy, sz, sd, st, hy, hz, hd,
    own_sem, kv_recv, kvz_send, kvy_send,
    tot_send, tot_recv, scan_send, scan_recv, red_send, red_recv, zy_send, zy_recv,
):
    c = lax.axis_index("ctx")
    d = lax.axis_index("dp")
    tt = lax.axis_index("tensor")
    z = c // ROW
    y = c % ROW

    def at_y(step):
        return {"ctx": z * ROW + (y + step) % ROW}

    def at_z(step):
        return {"ctx": ((z + step) % ROW) * ROW + y}

    def at_d(step):
        return {"dp": (d + step) % dp_size}

    def at_t(step):
        return {"tensor": (tt + step) % tensor_size}

    peers = [at_y(s) for s in range(1, ROW)] + [at_z(s) for s in range(1, ROW)]
    peers += [at_d(s) for s in range(1, dp_size)] + [at_t(s) for s in range(1, tensor_size)]

    zrecv[...] = jnp.zeros_like(zrecv)
    zrecv2[...] = jnp.zeros_like(zrecv2)

    barrier = pltpu.get_barrier_semaphore()
    for peer in peers:
        pl.semaphore_signal(barrier, inc=1, device_id=peer, device_id_type=MESH)

    def rows(slot):
        return pl.ds(pl.multiple_of(slot * T, T), T)

    own_k = pltpu.make_async_copy(k, kbuf.at[rows(c)], own_sem.at[0])
    own_v = pltpu.make_async_copy(v, vbuf.at[rows(c)], own_sem.at[1])
    loads = [
        pltpu.make_async_copy(src, dst, own_sem.at[2 + i])
        for i, (src, dst) in enumerate(((dt_in, dt), (bc_in, bc), (x_in, x), (q_in, q)))
    ]
    for copy in [own_k, own_v] + loads:
        copy.start()
    pl.semaphore_wait(barrier, len(peers))

    def remote(src, dst, send, recv, peer):
        return pltpu.make_async_remote_copy(
            src_ref=src, dst_ref=dst, send_sem=send, recv_sem=recv,
            device_id=peer, device_id_type=MESH,
        )

    bufs = (kbuf, vbuf)

    def kv_z(step, which):
        return remote(
            (k, v)[which], bufs[which].at[rows(c)], kvz_send.at[step - 1, which],
            kv_recv.at[which, c], at_z(step),
        )

    def kv_y(back, lane, which, slot, step):
        return remote(
            bufs[which].at[rows(slot)], bufs[which].at[rows(slot)], kvy_send.at[back, lane],
            kv_recv.at[which, slot], at_y(step),
        )

    def kv_wait(which, slot):
        remote(
            bufs[which].at[rows(slot)], bufs[which].at[rows(slot)], own_sem.at[which],
            kv_recv.at[which, slot], at_y(1),
        ).wait_recv()

    def y_sends(back):
        slot = (z - back) * ROW + y
        return [
            kv_y(back, 0, 0, slot, 1), kv_y(back, 1, 1, slot, 3),
            kv_y(back, 2, 1, slot, 1), kv_y(back, 3, 0, slot, 3),
        ]

    def slot_of(back, step):
        return (z - back) * ROW + (y + step) % ROW

    def forwards(back):
        return [kv_y(back, 4, 0, slot_of(back, 3), 1), kv_y(back, 5, 1, slot_of(back, 1), 3)]

    for step in (1, 2, 3):

        @pl.when(z + step < ROW)
        def _():
            for which in range(2):
                kv_z(step, which).start()

    own_k.wait()
    own_v.wait()
    for copy in y_sends(0):
        copy.start()

    def pass_down(back):
        for which in range(2):
            kv_wait(which, slot_of(back, 0))
        for copy in y_sends(back):
            copy.start()

    def pass_on(back):
        kv_wait(0, slot_of(back, 3))
        kv_wait(1, slot_of(back, 1))
        for copy in forwards(back):
            copy.start()

    def settle(back):
        kv_wait(1, slot_of(back, 3))
        kv_wait(0, slot_of(back, 1))
        for which in range(2):
            kv_wait(which, slot_of(back, 2))

    def group_cut(part, sub):
        g = 2 * part + sub
        return slice(g * 128, (g + 1) * 128)

    for copy in loads[:3]:
        copy.wait()
    bias = column(dtb)
    rate = jnp.exp(column(alog))
    shifted = dt[...] + bias
    step_size = jnp.maximum(shifted, 0.0) + jnp.log1p(jnp.exp(-jnp.abs(shifted)))
    decay = -step_size * rate
    upto = marks((T, T), lambda s, t: s <= t)
    same = marks((T, T), lambda s, t: s == t)
    cum_t = summed(nn, decay, upto)
    cum_c = summed(nt, cum_t, same, left=False)
    total = cum_t[:, T - 1 : T]
    cumt[...] = cum_t
    stept[...] = step_size
    spread = marks((HG, CH), lambda h, j: (j >> 6) == h)
    tail_step = jnp.exp(total - cum_t) * step_size
    ts_full[...] = summed(tn, tail_step, spread, 2)
    xs[...] = (ts_full[...] * x[...].astype(F32)).astype(BF16)
    pick_b = marks((T, 2 * T), lambda t, r: r == 2 * t)
    pick_c = marks((T, 2 * T), lambda t, r: r == 2 * t + 1)
    b_f = nn(pick_b, bc[...])
    c_f = nn(pick_c, bc[...])
    b_rows = b_f.astype(BF16)
    c_rows = c_f.astype(BF16)
    b_cols = b_f.T.astype(BF16)
    c_cols = c_f.T.astype(BF16)

    gate = 1.0 / (1.0 + jnp.exp(-shifted))
    later_than = marks((T, T), lambda s, t: s > t)
    gate_after = summed(nn, gate, later_than)
    gate_sum = jnp.broadcast_to(jnp.sum(gate, axis=1, keepdims=True) * rate, (HG, 128))
    gate_row = jnp.sum(
        jnp.where(iota((HG, 128), 1) == iota((HG, 128), 0) + HG, gate_sum, 0.0),
        axis=0, keepdims=True,
    )
    total_row = jnp.sum(
        jnp.where(
            iota((HG, 128), 1) == iota((HG, 128), 0), jnp.broadcast_to(total, (HG, 128)), 0.0
        ),
        axis=0, keepdims=True,
    )
    tot[pl.ds(c, 1)] = jnp.broadcast_to((total_row + gate_row)[None], (1, 8, 128))
    weight_z[...] = tail_step * (total - cum_t)
    weight_y[...] = tail_step * (gate / step_size - rate * gate_after)
    for sub in range(2):
        for part in range(4):
            ysend[sub, part] = nn(b_cols, xs[:, group_cut(part, sub)]).astype(BF16)

    def tot_y(step):
        return remote(
            tot.at[pl.ds(c, 1)], tot.at[pl.ds(c, 1)], tot_send.at[0, step - 1],
            tot_recv.at[0, y], at_y(step),
        )

    def tot_y_wait(step):
        other = (y + step) % ROW
        remote(
            tot.at[pl.ds(c, 1)], tot.at[pl.ds(z * ROW + other, 1)], tot_send.at[0, step - 1],
            tot_recv.at[0, other], at_y(step),
        ).wait_recv()

    def tot_z(step):
        return remote(
            tot.at[pl.ds(z * ROW, ROW)], tot.at[pl.ds(z * ROW, ROW)], tot_send.at[1, step - 1],
            tot_recv.at[1, z], at_z(step),
        )

    def tot_z_wait(step):
        other = (z + step) % ROW
        remote(
            tot.at[pl.ds(z * ROW, ROW)], tot.at[pl.ds(other * ROW, ROW)], tot_send.at[1, step - 1],
            tot_recv.at[1, other], at_z(step),
        ).wait_recv()

    def trade(phase, sub, src, dst, step):
        to = (y + step) % ROW
        return remote(
            src.at[sub, to], dst.at[sub, y], scan_send.at[phase, sub, step - 1],
            scan_recv.at[phase, sub, y], at_y(step),
        )

    def trade_wait(phase, sub, src, dst, step):
        other = (y + step) % ROW
        remote(
            src.at[sub, other], dst.at[sub, other], scan_send.at[phase, sub, step - 1],
            scan_recv.at[phase, sub, other], at_y(step),
        ).wait_recv()

    def climb(phase, sub, src, dst, step):
        return remote(
            src.at[sub], dst.at[sub, z], scan_send.at[phase, sub, step - 1],
            scan_recv.at[phase, sub, z], at_z(step),
        )

    def climb_wait(phase, sub, src, dst, step):
        other = (z + step) % ROW
        remote(
            src.at[sub], dst.at[sub, other], scan_send.at[phase, sub, step - 1],
            scan_recv.at[phase, sub, other], at_z(step),
        ).wait_recv()

    def trades(phase, sub, src, dst):
        for step in (2, 1, 3):
            trade(phase, sub, src, dst, step).start()
        dst[sub, pl.ds(y, 1)] = src[sub, pl.ds(y, 1)]

    for step in range(1, ROW):
        tot_y(step).start()
    for sub in range(2):
        trades(0, sub, ysend, yrecv)

    wmat[...] = nt(c_rows, b_rows)
    wtmat[...] = nt(b_rows, c_rows)
    step_c = summed(nt, step_size, same, left=False)
    for h in range(HG):
        cumb[:, h * 128 : (h + 1) * 128] = jnp.broadcast_to(cum_c[:, h : h + 1], (T, 128))
        stepb[:, h * 128 : (h + 1) * 128] = jnp.broadcast_to(step_c[:, h : h + 1], (T, 128))
    ecum_full[...] = summed(tn, jnp.exp(cum_t), spread, 2)

    low_half = iota((T, 128), 1) < 64
    zero_pair = jnp.zeros((T, 128), BF16)

    def halves(pair):
        return jnp.where(low_half, pair, zero_pair), jnp.where(low_half, zero_pair, pair)

    def lanes(index, width):
        return pl.ds(pl.multiple_of(index * width, width), width)

    def mix_pair(pair, carry):
        lower = iota((T, T), 0) >= iota((T, T), 1)
        upper = iota((T, T), 0) <= iota((T, T), 1)
        parts = halves(x[:, lanes(pair, 128)])
        result = jnp.zeros((T, 128), F32)
        for i in range(2):
            h = 2 * pair + i
            at_t = cumb[:, lanes(h, 128)]
            at_t = jnp.concatenate([at_t, at_t], axis=1)
            size_c = stepb[:, lanes(h, 128)]
            size_c = jnp.concatenate([size_c, size_c], axis=1)
            at_s = cumt[pl.ds(h, 1), :]
            size_r = stept[pl.ds(h, 1), :]
            held = jnp.exp(jnp.where(lower, at_t - at_s, NEGATIVE)) * size_r
            timed[h] = held
            mixed = (held * wmat[...]).astype(BF16)
            result = result + nn(mixed, parts[i])
            turned = jnp.exp(jnp.where(upper, at_s - at_t, NEGATIVE)) * size_c
            mixt[h] = (turned * wtmat[...]).astype(BF16)
        intra[:, lanes(pair, 128)] = result
        return carry


    @pl.when(z >= 1)
    def _():
        pass_down(1)

    pass_on(0)
    lax.fori_loop(0, GROUP // 2, mix_pair, 0, unroll=2)
    for step in range(1, ROW):
        tot_y_wait(step)
    for step in range(1, ROW):
        tot_z(step).start()
    lax.fori_loop(GROUP // 2, GROUP, mix_pair, 0, unroll=2)


    @pl.when(z >= 2)
    def _():
        pass_down(2)
    mine = marks((128, QW), lambda h, j: h == y * 4 + (j >> 6))
    mine_next = marks((128, QW), lambda h, j: h == HG + y * 4 + (j >> 6))
    row_tot = jnp.sum(
        jnp.where(iota((ROW, 8, 128), 1) == 0, tot[pl.ds(z * ROW, ROW)], 0.0), axis=1
    )
    row_tot = jnp.concatenate([row_tot, row_tot], axis=0)
    own_tot = summed(nn, row_tot, mine)
    own_gate = summed(nn, row_tot, mine_next)
    for sub in range(2):
        tqo[sub] = own_tot[:, sub * 128 : (sub + 1) * 128]
        gqo[sub] = own_gate[:, sub * 128 : (sub + 1) * 128]

    def own_total(sub, kk):
        return tqo[sub, kk : kk + 1, :]

    def total_of(sub, zz, kk):
        return tq[sub, zz * ROW + kk : zz * ROW + kk + 1, :]

    def row_total(sub, zz):
        return sum(total_of(sub, zz, kk) for kk in range(1, ROW)) + total_of(sub, zz, 0)

    def scan_row(phase, sub, src, got, up, pre, order):
        for step in range(1, ROW):
            trade_wait(phase, sub, src, got, step)
        run = jnp.zeros((N, 128), F32)
        for kk in order:
            pre[sub, kk] = run
            run = jnp.exp(own_total(sub, kk)) * run + got[sub, kk].astype(F32)
        up[sub] = run.astype(BF16)

    def scan_back(phase, sub, got, back, final, pre, order, rows_in, arrived):
        held = jnp.zeros((N, 128), F32)
        for zz in rows_in:
            held = jnp.where(
                arrived(zz), jnp.exp(row_total(sub, zz)) * held + got[sub, zz].astype(F32), held
            )
        passed = jnp.zeros((1, 128), F32)
        for kk in order:
            back[sub, kk] = (jnp.exp(passed) * held + pre[sub, kk]).astype(BF16)
            passed = passed + own_total(sub, kk)
        trades(phase, sub, back, final)

    def tiles(a):
        return jnp.sum(a.reshape(N // 8, 8, 128), axis=0)

    def functionals(sub):
        for_decay = jnp.zeros((8, 128), F32)
        for_shift = jnp.zeros((8, 128), F32)
        for kk in range(ROW):
            later = bsend2[sub, kk].astype(F32)
            sofar = own_total(sub, kk)
            met = jnp.exp(sofar) * tiles(later * bsend[sub, kk].astype(F32))
            gates = gqo[sub, kk : kk + 1, :]
            for_decay = for_decay + tiles(later * zyrecv[kk, 2 * sub].astype(F32)) + sofar * met
            for_shift = for_shift + tiles(later * zyrecv[kk, 2 * sub + 1].astype(F32)) - gates * met
        return for_decay, for_shift

    ahead = (0, 1, 2, 3)
    behind = (3, 2, 1, 0)
    for sub in range(2):
        scan_row(0, sub, ysend, yrecv, zsend, before, ahead)
        for step in range(1, ROW):

            @pl.when(z + step < ROW)
            def _():
                climb(1, sub, zsend, zrecv, step).start()

    ones = jnp.ones((ROW * T, HD), BF16)

    def attend(row, first, heads):
        base = pl.multiple_of(row * (ROW * T), ROW * T)
        start, stride, count = heads

        def one(i, carry):
            g = start + stride * i
            keys = kbuf[pl.ds(base, ROW * T), :]
            both = jnp.concatenate([vbuf[pl.ds(base, ROW * T), :], ones], axis=1)
            scores = nt(q[:, lanes(g, HD)], keys)
            if first:
                seen = iota((T, ROW * T), 1) <= iota((T, ROW * T), 0) + y * T
                scores = jnp.where(seen, scores, NEGATIVE)
            top = jnp.max(scores, axis=1, keepdims=True)
            if first:
                new = jnp.broadcast_to(top, (T, HD))
            else:
                old = m_ref[g]
                new = jnp.maximum(old, top)
            weights = jnp.exp2((scores - jnp.concatenate([new] * 8, axis=1)) * EXP_SCALE)
            part = nn(weights.astype(BF16), both)
            if first:
                acc[g] = part
            else:
                scale = jnp.exp2((old - new) * EXP_SCALE)
                acc[g] = acc[g] * jnp.concatenate([scale, scale], axis=1) + part
            m_ref[g] = new
            return carry

        lax.fori_loop(0, count, one, 0, unroll=4)

    all_heads = (0, 1, GROUP)
    loads[3].wait()

    @pl.when(z >= 3)
    def _():
        pass_down(3)

    settle(0)
    attend(z, True, (0, 2, GROUP // 2))

    @pl.when(z >= 1)
    def _():
        pass_on(1)

    attend(z, True, (1, 2, GROUP // 2))

    @pl.when(z >= 2)
    def _():
        pass_on(2)
        settle(1)
        attend(z - 1, False, (0, 2, GROUP // 2))

    @pl.when(z >= 3)
    def _():
        pass_on(3)

    @pl.when(z >= 2)
    def _():
        attend(z - 1, False, (1, 2, GROUP // 2))

    for step in range(1, ROW):
        tot_z_wait(step)
    totals = jnp.sum(jnp.where(iota((16, 8, 128), 1) == 0, tot[...], 0.0), axis=1)
    all_tot = summed(nn, totals, mine)
    for sub in range(2):
        tq[sub] = all_tot[:, sub * 128 : (sub + 1) * 128]

    for sub in range(2):
        for step in range(1, ROW):

            @pl.when(z >= step)
            def _():
                climb_wait(1, sub, zsend, zrecv, ROW - step)

        scan_back(2, sub, zrecv, bsend, brecv, before, ahead, (0, 1, 2), lambda zz: zz < z)

    @pl.when(z >= 3)
    def _():
        settle(2)
        attend(z - 2, False, all_heads)

    for sub in range(2):
        for step in range(1, ROW):
            trade_wait(2, sub, bsend, brecv, step)
        for part in range(4):
            cut = group_cut(part, sub)
            inter[:, cut] = ecum_full[:, cut] * nn(c_rows, brecv[sub, part])

    @pl.when(z >= 1)
    def _():
        settle(z)

    skip_row = summed(nn, jnp.broadcast_to(skp[...], (8, HG)), spread)[0:1, :]

    def fold(a):
        a = a.reshape(T // 8, 8, a.shape[1])
        a = jnp.sum(a, axis=0)
        out = a[:, 0:128]
        for j in range(1, a.shape[1] // 128):
            out = out + a[:, j * 128 : (j + 1) * 128]
        return out

    def rise(sub):
        scan_row(3, sub, ysend2, yrecv2, zsend2, before, behind)
        for step in range(1, ROW):

            @pl.when(z >= step)
            def _():
                climb(4, sub, zsend2, zrecv2, ROW - step).start()

    power = jnp.zeros((8, 128), F32)
    error = jnp.zeros((8, 128), F32)
    for sub in range(2):

        @pl.when(z >= 1)
        def _():
            attend(0, False, (sub, 2, GROUP // 2))

        for part in range(4):
            cut = group_cut(part, sub)
            both = acc[2 * part + sub]
            goal = (both[:, :HD] / both[:, HD:]).astype(BF16).astype(F32)
            made = intra[:, cut] + inter[:, cut] + skip_row[:, cut] * x[:, cut].astype(F32)
            resid = made - goal
            power = power + fold(goal * goal)
            error = error + fold(resid * resid)
            up = 2.0 * resid
            ups[:, cut] = up
            upb[:, cut] = up.astype(BF16)
            eu[:, cut] = (ecum_full[:, cut] * up).astype(BF16)
            ysend2[sub, part] = nn(c_cols, eu[:, cut]).astype(BF16)
        trades(3, sub, ysend2, yrecv2)

    def spread_out(buf, place, stage, at, size):
        out = []
        for step in range(1, size):
            out.append(
                remote(
                    buf.at[pl.ds(place, 1)], buf.at[pl.ds(place, 1)], red_send.at[stage, step - 1],
                    red_recv.at[stage, place], at(step),
                )
            )
        return out

    def collect(buf, place, stage, at, size):
        for step in range(1, size):
            other = (place + step) % size
            remote(
                buf.at[pl.ds(place, 1)], buf.at[pl.ds(other, 1)], red_send.at[stage, step - 1],
                red_recv.at[stage, other], at(step),
            ).wait_recv()
        total = buf[0]
        for j in range(1, size):
            total = total + buf[j]
        return total

    def launch(value, buf, place, stage, at, size):
        buf[pl.ds(place, 1)] = value[None]
        for copy in spread_out(buf, place, stage, at, size):
            copy.start()

    launch(jnp.concatenate([power, error], axis=0), sd, d, 2, at_d, dp_size)
    for kind, weight in enumerate((weight_z, weight_y)):
        eu_like[...] = (summed(tn, weight[...], spread, 2) * x[...].astype(F32)).astype(BF16)
        for sub in range(2):
            for part in range(4):
                zysend[part, 2 * sub + kind] = nn(
                    b_cols, eu_like[:, group_cut(part, sub)]
                ).astype(BF16)

    def zy(step):
        to = (y + step) % ROW
        return remote(
            zysend.at[to], zyrecv.at[y], zy_send.at[step - 1], zy_recv.at[y], at_y(step)
        )

    def zy_wait(step):
        other = (y + step) % ROW
        remote(
            zysend.at[other], zyrecv.at[other], zy_send.at[step - 1], zy_recv.at[other], at_y(step)
        ).wait_recv()

    for step in range(1, ROW):
        zy(step).start()
    zyrecv[pl.ds(y, 1)] = zysend[pl.ds(y, 1)]

    rise(0)
    rise(1)
    launch(collect(sd, d, 2, at_d, dp_size), st, tt, 3, at_t, tensor_size)

    def pair_products(pair, running):
        ups_pair = halves(upb[:, lanes(pair, 128)])
        x_pair = x[:, lanes(pair, 128)]
        through = jnp.zeros((T, 128), F32)
        for i in range(2):
            h = 2 * pair + i
            running = running + timed[h] * nt(ups_pair[i], x_pair)
            through = through + nn(mixt[h], ups_pair[i])
        t1[:, lanes(pair, 128)] = through
        return running

    paired = lax.fori_loop(0, GROUP, pair_products, jnp.zeros((T, T), F32), unroll=2)

    def by_head(a):
        return summed(nt, a, spread, 2, left=False)

    heads_at = marks((CH, 128), lambda j, h: (j >> 6) == h)
    heads_next = marks((CH, 128), lambda j, h: (j >> 6) == h - HG)
    xf = x[...].astype(F32)
    through_x = xf * t1[...]
    gains = upb[...].astype(F32) * intra[...] - through_x + ups[...] * inter[...]
    stats = summed(nn, gains, heads_at, 2) + nn(through_x.astype(BF16), heads_next)
    stats = stats.T
    gained = stats[0:HG]
    from_mix = stats[HG : 2 * HG]
    skip_part = jnp.sum((ups[...] * xf).reshape(T // 8, 8, CH), axis=0)
    skip_term = jnp.sum(by_head(skip_part), axis=1, keepdims=True)
    since = marks((T, T), lambda s, t: s >= t)
    until = marks((T, T), lambda s, t: s < t)
    gained_after = summed(nn, gained, since)
    decay_local = jnp.sum(gained_after * decay, axis=1, keepdims=True)
    shift_local = jnp.sum(
        (from_mix / step_size - gained_after * rate) * gate, axis=1, keepdims=True
    )
    paired_rows = paired.astype(BF16)
    paired_cols = paired.T.astype(BF16)
    grad_b = nn(paired_cols, c_rows)
    grad_c = nn(paired_rows, b_rows)
    for sub in range(2):
        for part in range(4):
            grad_c = grad_c + nt(eu[:, group_cut(part, sub)], brecv[sub, part])

    launch(collect(st, tt, 3, at_t, tensor_size), sz, z, 1, at_z, ROW)

    for step in range(1, ROW):
        zy_wait(step)
    for sub in range(2):
        for step in range(1, ROW):

            @pl.when(z + step < ROW)
            def _():
                climb_wait(4, sub, zsend2, zrecv2, step)

        scan_back(5, sub, zrecv2, bsend2, brecv2, before, behind, (3, 2, 1), lambda zz: zz > z)
    parts = [functionals(0), functionals(1)]
    owned = marks((HG, QW), lambda h, j: h == y * 4 + (j >> 6))

    def owned_heads(kind):
        both = jnp.concatenate([parts[0][kind], parts[1][kind]], axis=1)
        return jnp.sum(summed(nt, both, owned, left=False), axis=1, keepdims=True)

    lane = iota((HG, 128), 1)
    heads = jnp.where(
        lane == 0, decay_local + owned_heads(0),
        jnp.where(lane == 1, shift_local + owned_heads(1), skip_term),
    )
    launch(heads, hd, d, 6, at_d, dp_size)

    launch(collect(sz, z, 1, at_z, ROW), sy, y, 0, at_y, ROW)
    launch(collect(hd, d, 6, at_d, dp_size), hz, z, 5, at_z, ROW)
    overlap = [None] * 8
    later_stats = jnp.zeros((T, 128), F32)
    for sub in range(2):
        for step in range(1, ROW):
            trade_wait(5, sub, bsend2, brecv2, step)
        for part in range(4):
            cut = group_cut(part, sub)
            later = brecv2[sub, part]
            came = ts_full[:, cut] * nn(b_rows, later)
            inter[:, cut] = skip_row[:, cut] * ups[:, cut] + t1[:, cut] + came
            grad_b = grad_b + nt(xs[:, cut], later)
            later_stats = later_stats + nn(
                (x[:, cut].astype(F32) * came).astype(BF16), heads_at[cut, :]
            )
            prod = later.astype(F32) * brecv[sub, part].astype(F32)
            overlap[2 * part + sub] = tiles(prod)
        if sub == 0:
            launch(collect(hz, z, 5, at_z, ROW), hy, y, 4, at_y, ROW)
    from_later = later_stats.T[0:HG]
    meet = jnp.sum(by_head(jnp.concatenate(overlap, axis=1)), axis=1, keepdims=True)
    decay_grad = gained_after + summed(nn, from_later, until) + jnp.exp(total) * meet
    direct = (from_mix + from_later) / step_size
    shift_grad = (direct - decay_grad * rate) * gate
    both_sums = collect(sy, y, 0, at_y, ROW)
    power_all = jnp.sum(both_sums[0:8, :], keepdims=True)
    error_all = jnp.sum(both_sums[8:16, :], keepdims=True)
    mean_square = power_all / entries + EPSILON
    factor = 1.0 / mean_square
    gls[...] = jnp.broadcast_to(error_all / mean_square / entries, (8, 128))

    gx[...] = (inter[...] * factor).astype(BF16)
    gdt[...] = shift_grad * factor
    put_b = marks((2 * T, T), lambda r, t: r == 2 * t)
    put_c = marks((2 * T, T), lambda r, t: r == 2 * t + 1)
    gbc[...] = (
        nn(put_b, (grad_b * factor).astype(BF16)) + nn(put_c, (grad_c * factor).astype(BF16))
    ).astype(BF16)
    ghd[...] = collect(hy, y, 4, at_y, ROW) * factor

    for step in range(1, ROW):

        @pl.when(z + step < ROW)
        def _():
            for which in range(2):
                kv_z(step, which).wait_send()
            for sub in range(2):
                climb(1, sub, zsend, zrecv, step).wait_send()

        @pl.when(z >= step)
        def _():
            for sub in range(2):
                climb(4, sub, zsend2, zrecv2, ROW - step).wait_send()

        zy(step).wait_send()
        tot_y(step).wait_send()
        tot_z(step).wait_send()
        for sub in range(2):
            trade(0, sub, ysend, yrecv, step).wait_send()
            trade(2, sub, bsend, brecv, step).wait_send()
            trade(3, sub, ysend2, yrecv2, step).wait_send()
            trade(5, sub, bsend2, brecv2, step).wait_send()
    for back in range(ROW):

        @pl.when(z >= back)
        def _():
            for copy in y_sends(back) + forwards(back):
                copy.wait_send()

    for buf, place, stage, at, size in (
        (sy, y, 0, at_y, ROW), (sz, z, 1, at_z, ROW), (sd, d, 2, at_d, dp_size),
        (st, tt, 3, at_t, tensor_size), (hy, y, 4, at_y, ROW), (hz, z, 5, at_z, ROW),
        (hd, d, 6, at_d, dp_size),
    ):
        for copy in spread_out(buf, place, stage, at, size):
            copy.wait_send()


def write_out(gx, gbc, gdt, ghd, gls, ogx, ogbc, ogdt, oghd, ogls):
    ogx[...] = gx[...]
    ogbc[...] = gbc[...]
    ogdt[...] = gdt[...]
    turned = ghd[...].T
    for i in range(3):
        oghd[i] = turned[i : i + 1, :]
    ogls[...] = gls[0:1, 0:1]


def solution(mesh):
    dp_size, tensor_size = mesh.shape["dp"], mesh.shape["tensor"]
    entries = float(dp_size * mesh.shape["ctx"] * tensor_size * T * CH)

    def vm(shape, kind):
        return pltpu.VMEM(shape, kind)

    chunk4 = (2, ROW, N, 128)
    scratch = [
        vm((T, CH), BF16), vm((T, CH), BF16), vm((2 * T, N), BF16), vm((HG, T), F32),
        vm((16 * T, HD), BF16), vm((16 * T, HD), BF16),
        vm((GROUP, T, HD), F32), vm((GROUP, T, 2 * HD), F32),
        vm((HG, T, T), F32), vm((HG, T, T), BF16),
        vm((T, HG * 128), F32), vm((T, HG * 128), F32),
        vm((HG, T), F32), vm((HG, T), F32), vm((T, T), F32), vm((T, T), F32),
        vm((T, CH), F32), vm((T, CH), F32), vm((T, CH), BF16), vm((T, CH), F32),
        vm((T, CH), F32), vm((T, CH), F32), vm((T, CH), BF16), vm((T, CH), BF16),
        vm((T, CH), F32),
        vm((16, 8, 128), F32), vm((2, 16, 128), F32), vm((2, 8, 128), F32), vm((2, 8, 128), F32),
        vm((2, ROW, N, 128), F32),
        vm((HG, T), F32), vm((HG, T), F32), vm((T, CH), BF16),
        vm((ROW, 4, N, 128), BF16), vm((ROW, 4, N, 128), BF16),
    ]
    for _ in range(2):
        scratch += [
            vm(chunk4, BF16), vm(chunk4, BF16), vm((2, N, 128), BF16), vm(chunk4, BF16),
            vm(chunk4, BF16), vm(chunk4, BF16),
        ]
    scratch += [
        vm((ROW, 16, 128), F32), vm((ROW, 16, 128), F32), vm((dp_size, 16, 128), F32),
        vm((tensor_size, 16, 128), F32), vm((ROW, 16, 128), F32), vm((ROW, 16, 128), F32),
        vm((dp_size, 16, 128), F32),
    ]
    sem = pltpu.SemaphoreType.DMA
    scratch += [
        sem((6,)), sem((2, 16)), sem((3, 2)), sem((4, 6)),
        sem((2, 3)), sem((2, 4)), sem((6, 2, 3)), sem((6, 2, 4)), sem((7, 3)), sem((7, 4)), sem((3,)), sem((4,)),
    ]

    def body(queries, keys, values, student_x, student_bc, student_dt, a_log, dt_bias, skip):
        whole = pl.BlockSpec(memory_space=pltpu.VMEM)
        far = pl.BlockSpec(memory_space=pltpu.HBM)

        def run(*refs):
            kernel(entries, dp_size, tensor_size, *refs)

        gx, gbc, gdt, ghd, gls = pl.pallas_call(
            run,
            out_shape=(
                jax.ShapeDtypeStruct((T, CH), BF16),
                jax.ShapeDtypeStruct((2 * T, N), BF16),
                jax.ShapeDtypeStruct((HG, T), F32),
                jax.ShapeDtypeStruct((HG, 128), F32),
                jax.ShapeDtypeStruct((8, 128), F32),
            ),
            in_specs=[far] * 6 + [whole] * 3,
            out_specs=(whole,) * 5,
            scratch_shapes=scratch,
            compiler_params=pltpu.CompilerParams(
                collective_id=0, has_side_effects=True, vmem_limit_bytes=61 * 1024 * 1024
            ),
            name="align",
        )(
            queries.reshape(T, CH), keys.reshape(T, HD), values.reshape(T, HD),
            student_x.reshape(T, CH), student_bc.reshape(2 * T, N),
            student_dt.reshape(T, HG).T, a_log, dt_bias, skip,
        )
        gx, gbc, gdt, ghd, gls = pl.pallas_call(
            write_out,
            out_shape=(
                jax.ShapeDtypeStruct((T, CH), BF16),
                jax.ShapeDtypeStruct((2 * T, N), BF16),
                jax.ShapeDtypeStruct((HG, T), F32),
                jax.ShapeDtypeStruct((3, 1, HG), F32),
                jax.ShapeDtypeStruct((1, 1), F32),
            ),
            in_specs=[whole] * 5,
            out_specs=(whole,) * 5,
            compiler_params=pltpu.CompilerParams(vmem_limit_bytes=61 * 1024 * 1024),
            name="write_out",
        )(gx, gbc, gdt, ghd, gls)
        return (
            gx.reshape(1, T, 1, CH),
            gbc.reshape(1, T, 1, 2, N),
            gdt.T.reshape(1, T, 1, HG),
            ghd,
            gls.reshape(()),
        )

    return jax.shard_map(
        body,
        mesh=mesh,
        in_specs=(
            P("dp", "ctx", "tensor", None),
            P("dp", "ctx", "tensor", None),
            P("dp", "ctx", "tensor", None),
            P("dp", "ctx", "tensor", None),
            P("dp", "ctx", "tensor", None, None),
            P("dp", "ctx", "tensor", None),
            P("tensor", None),
            P("tensor", None),
            P("tensor", None),
        ),
        out_specs=(
            P("dp", "ctx", "tensor", None),
            P("dp", "ctx", "tensor", None, None),
            P("dp", "ctx", "tensor", None),
            P(None, "tensor", None),
            P(),
        ),
        check_vma=False,
    )
```
